32 devices in a mesh: groups: 2 (over y), seq: 8 (over z, x), chan: 2 (over core).
Axes of the slice: x: 2, y: 2, z: 4, core: 2. Of those that a mesh axis runs over, the one named last changes fastest.
Arguments:
- projected: bfloat16 [3, 2048, 1024], P(None, ('groups', 'seq'), 'chan'), parts along dimension 1, may hold values from -6 to 6
- long_filter: float32 [2048, 1024], P(('groups', 'seq'), 'chan'), parts along dimension 0, may hold values from -6 to 6
- short_kernel: float32 [3, 7, 1024], P(None, None, 'chan'), may hold values from -2 to 2
- skip_gain: float32 [1024], P('chan'), may hold values from 0.25 to 1.5
- cotangent: bfloat16 [2048, 1024], P(('groups', 'seq'), 'chan'), parts along dimension 0, may hold values from -6 to 6
Outputs:
- layer_output: bfloat16 [2048, 1024], P(('groups', 'seq'), 'chan'), parts along dimension 0
- stream_grads: bfloat16 [3, 2048, 1024], P(None, ('groups', 'seq'), 'chan'), parts along dimension 1
- filter_grad: float32 [2048, 1024], P(('groups', 'seq'), 'chan'), parts along dimension 0
- kernel_grad: float32 [6, 7, 1024], P('groups', None, 'chan'), parts along dimension 0
- skip_grad: float32 [2048], P(('groups', 'chan')), parts along dimension 0
The draws below stay inside these ranges and needn't reach their ends.
There are 2 independent parts, one for each index of `groups`. The reference program is written for one: setup_inputs(seed, part) draws one part's arguments, and reference() takes and returns one part's arrays. A program takes and returns all parts, laid end to end along the dimension named above; an argument that names none is the same for every part. Nothing has to cross between parts.
All inputs are finite; a program needn't handle non-finite values.
Results may differ from the reference program's by a relative error of at most 0.001.
Values may be sent and summed in bfloat16 or wider, within the bound.
A program may use at most 64 MiB of HBM per device.

```python
import math
import jax
import jax.numpy as jnp

D = 1024
TAPS = 7
TOKENS = 1024


def block_scale(stream_key, dims, pieces, low, high):
    loudness = 1.0
    for position, blocks in pieces:
        heights = jax.random.uniform(jax.random.fold_in(jax.random.fold_in(stream_key, 6), position), (blocks,), jnp.float32, low / len(pieces), high / len(pieces))
        loudness = loudness * jnp.repeat(jnp.exp(heights), dims[position] // blocks).reshape((-1,) + (1,) * (len(dims) - 1 - position))
    return loudness


def gaussian(key, shape, width, limit, shards=(), held_as=jnp.bfloat16):
    values = jax.random.normal(key, shape, jnp.float32) * width
    if len(shards) > 0:
        values = block_scale(key, shape, shards, -0.22, 0.18) * values
    return jnp.clip(values, min=-limit, max=limit).astype(held_as)


def setup_inputs(seed: int = 0, part: int = 0) -> dict:
    keys = jax.random.split(jax.random.key(seed), 6)
    own_keys = jax.random.split(jax.random.fold_in(keys[5], part), 6)
    projected = gaussian(own_keys[0], (3, TOKENS, D), 1.0, 6.0, ((1, 8), (2, 2)))
    long_filter = gaussian(own_keys[1], (TOKENS, D), 1.0, 6.0, ((0, 8), (1, 2)), jnp.float32)
    short_kernel = gaussian(keys[2], (3, TAPS, D), TAPS ** -0.5, 2.0, ((2, 2),), jnp.float32)
    skip_gain = jnp.clip(0.25 + 1.25 * jax.random.uniform(keys[3], (D,), jnp.float32) ** block_scale(keys[3], (D,), ((0, 2),), -0.2, 0.2), 0.25, 1.5)
    cotangent = gaussian(own_keys[4], (TOKENS, D), 1.0, 6.0, ((0, 8), (1, 2)))
    return {"projected": projected, "long_filter": long_filter, "short_kernel": short_kernel, "skip_gain": skip_gain, "cotangent": cotangent}


def circular_taps(streams, short_kernel):
    margin = short_kernel.shape[1] // 2
    summed = jnp.zeros(streams.shape, jnp.float32)
    for offset in range(short_kernel.shape[1]):
        summed = summed + short_kernel[:, offset][:, None, :] * jnp.roll(streams, margin - offset, axis=1)
    return summed

def long_layer(streams, long_filter, short_kernel, skip_gain):
    factor = 1.0 / math.sqrt(TOKENS)
    shorts = circular_taps(streams, short_kernel)
    gated_signal = shorts[1] * shorts[2]
    spectrum = jnp.fft.rfft(gated_signal, axis=0) * jnp.fft.rfft(long_filter * factor, axis=0)
    response = jnp.fft.irfft(spectrum, n=TOKENS, axis=0) + skip_gain * gated_signal
    return response * shorts[0]

def reference(projected, long_filter, short_kernel, skip_gain, cotangent):
    streams = projected.astype(jnp.float32)
    output, pullback = jax.vjp(long_layer, streams, long_filter, short_kernel, skip_gain)
    stream_part, filter_part, kernel_part, skip_part = pullback(cotangent.astype(jnp.float32))
    factor = 1.0 / math.sqrt(TOKENS)
    return (output.astype(jnp.bfloat16), stream_part.astype(jnp.bfloat16), filter_part, kernel_part * factor, skip_part * factor)
```

```python
import functools
import math

import jax
import jax.numpy as jnp
import numpy as np
from jax import lax
from jax.experimental import pallas as pl
from jax.experimental.pallas import tpu as pltpu
from jax.sharding import PartitionSpec as P

HIGHEST = lax.Precision.HIGHEST
LANES = 128
HALF = LANES // 2
RIM = 8


def turned(value, step, extent):
    real_part, imaginary = value
    step = step % extent
    if step == 0:
        return value
    if 2 * step == extent:
        return (-real_part, None if imaginary is None else -imaginary)
    if 4 * step == extent:
        return (None if imaginary is None else -imaginary, real_part)
    if 4 * step == 3 * extent:
        return (imaginary, -real_part)
    cosine = math.cos(2.0 * math.pi * step / extent)
    sine = math.sin(2.0 * math.pi * step / extent)
    if imaginary is None:
        return (real_part * cosine, real_part * sine)
    return (real_part * cosine - imaginary * sine, imaginary * cosine + real_part * sine)


def part_sum(left, right, sign):
    if right is None:
        return left
    if left is None:
        return right if sign > 0 else -right
    return left + right if sign > 0 else left - right


def real_spectrum(values):
    extent = len(values)
    if extent == 2:
        return [(values[0] + values[1], None), (values[0] - values[1], None)]
    even, odd = real_spectrum(values[0::2]), real_spectrum(values[1::2])
    half = extent // 2

    def entry(spectrum, index):
        index = index % half
        if 2 * index <= half:
            return spectrum[index]
        real_part, imaginary = spectrum[half - index]
        return (real_part, None if imaginary is None else -imaginary)

    found = []
    for index in range(half + 1):
        left, right = entry(even, index), turned(entry(odd, index), -index, extent)
        found.append((part_sum(left[0], right[0], 1), part_sum(left[1], right[1], 1)))
    return found


def real_values(spectrum):
    extent = 2 * (len(spectrum) - 1)
    if extent == 2:
        first, last = spectrum[0][0], spectrum[1][0]
        return [first + last, first - last]
    half = extent // 2
    even, odd = [], []
    for index in range(half // 2 + 1):
        real_part, imaginary = spectrum[index]
        if 2 * index == half:
            even.append((2.0 * real_part, None))
            odd.append((-2.0 * imaginary, None))
            continue
        other_real, other_imag = spectrum[half - index]
        even.append(
            (real_part + other_real, part_sum(imaginary, other_imag, -1))
        )
        odd.append(
            turned(
                (real_part - other_real, part_sum(imaginary, other_imag, 1)), index, extent
            )
        )
    found = [None] * extent
    found[0::2] = real_values(even)
    found[1::2] = real_values(odd)
    return found


def fine_tables(slabs, width):
    extent = slabs * width
    coarse = np.arange(slabs // 2 + 1)[:, None, None]
    fine = np.arange(width)[None, :, None]
    place = np.arange(width)[None, None, :]
    angles = ((coarse + slabs * fine) * place % extent) * (2.0 * np.pi / extent)
    cosine, sine = np.cos(angles), np.sin(angles)
    table = np.concatenate(
        [np.concatenate([cosine, sine], 2), np.concatenate([-sine, cosine], 2)], 1
    )
    inverse = np.swapaxes(table, 1, 2) / (extent * math.sqrt(extent))
    return table.astype(np.float32), inverse.astype(np.float32)


def layer_kernel(
    devices,
    projected_ref,
    filter_ref,
    taps_ref,
    gain_ref,
    cotangent_ref,
    forward_ref,
    inverse_ref,
    output_ref,
    streams_ref,
    filter_grad_ref,
    taps_grad_ref,
    gain_grad_ref,
    send_pairs,
    recv_pairs,
    send_filter,
    recv_filter,
    send_grads,
    recv_grads,
    send_response,
    recv_response,
    send_sums,
    recv_sums,
    first_rim,
    second_rim,
    first_short,
    second_short,
    signal,
    spectra,
    send_sem,
    recv_sem,
):
    rows = projected_ref.shape[1]
    span = taps_ref.shape[1]
    margin = span // 2
    width = rows // 2
    slabs = 2 * devices
    extent = rows * devices
    factor = 1.0 / math.sqrt(extent)
    tiles = devices // 2
    me = lax.axis_index("seq")
    odd = lax.rem(me, 2) == 1

    def low_lanes(shape):
        return lax.broadcasted_iota(jnp.int32, shape, 1) < HALF

    def swap(value):
        return pltpu.roll(value, HALF, 1)

    def join(first, second, parity):
        low = low_lanes(first.shape)
        if parity == 0:
            return jnp.where(low, first, swap(second))
        return jnp.where(low, swap(first), second)

    def wide(value):
        return value.astype(jnp.float32)

    def copy_to(kind, hop, source, target, slot, peer):
        return pltpu.make_async_remote_copy(
            src_ref=source,
            dst_ref=target.at[slot],
            send_sem=send_sem.at[kind, hop],
            recv_sem=recv_sem.at[kind, hop],
            device_id={"seq": peer},
            device_id_type=pl.DeviceIdType.MESH,
        )

    def peer_at(hop):
        return lax.rem(me + hop, devices)

    def source_at(hop):
        return lax.rem(me + devices - hop, devices)

    barrier = pltpu.get_barrier_semaphore()
    for hop in range(1, devices):
        pl.semaphore_signal(
            barrier, inc=1, device_id={"seq": peer_at(hop)}, device_id_type=pl.DeviceIdType.MESH
        )

    for tile in range(tiles):
        lanes = slice(tile * LANES, (tile + 1) * LANES)
        gate, left, right = [wide(projected_ref[s, :, lanes]) for s in range(3)]
        upstream = wide(cotangent_ref[:, lanes])
        for parity in range(2):
            send_pairs[2 * tile + parity, 0] = join(left, gate, parity).astype(jnp.bfloat16)
            send_pairs[2 * tile + parity, 1] = join(right, upstream, parity).astype(jnp.bfloat16)
    pl.semaphore_wait(barrier, devices - 1)
    for hop in range(1, devices):
        peer = peer_at(hop)
        copy_to(0, hop, send_pairs.at[peer], recv_pairs, me, peer).start()
    for tile in range(tiles):
        lanes = slice(tile * LANES, (tile + 1) * LANES)
        whole = filter_ref[:, lanes]
        coarse = wide(whole.astype(jnp.bfloat16))
        for parity in range(2):
            send_filter[2 * tile + parity] = join(coarse, whole - coarse, parity).astype(
                jnp.bfloat16
            )
    for hop in range(1, devices):
        peer = peer_at(hop)
        copy_to(1, hop, send_filter.at[peer], recv_filter, me, peer).start()
    recv_pairs[me] = send_pairs[me]
    recv_filter[me] = send_filter[me]

    own = pl.ds(pl.multiple_of((me // 2) * LANES, LANES), LANES)

    def own_pair(first, second):
        return jnp.where(odd, join(first, second, 1), join(first, second, 0))

    gate_taps, left_taps, right_taps = [taps_ref[s, :, own] for s in range(3)]
    first_taps = own_pair(left_taps, gate_taps)
    centre = wide(lax.broadcasted_iota(jnp.int32, (span, LANES), 0) == margin)
    second_taps = jnp.where(
        low_lanes((span, LANES)), own_pair(right_taps, right_taps), centre
    )
    own_gain = gain_ref[:, own]
    gain = own_pair(own_gain, own_gain)

    def wait_from(kind, source, target):
        for hop in range(1, devices):
            copy_to(kind, hop, source.at[peer_at(hop)], target, source_at(hop), peer_at(hop)).wait()

    def close_rim(rim):
        rim[0:RIM] = rim[extent : extent + RIM]
        rim[extent + RIM : extent + 2 * RIM] = rim[RIM : 2 * RIM]

    wait_from(0, send_pairs, recv_pairs)
    for block in range(devices):
        here = slice(RIM + block * rows, RIM + (block + 1) * rows)
        first_rim[0, here] = wide(recv_pairs[block, 0])
        second_rim[0, here] = wide(recv_pairs[block, 1])
    close_rim(first_rim.at[0])
    close_rim(second_rim.at[0])

    def shorten(slab, total):
        start = pl.multiple_of(slab * width, width)
        around_first = first_rim[0, pl.ds(start, width + 2 * RIM)]
        around_second = second_rim[0, pl.ds(start, width + 2 * RIM)]
        first = jnp.zeros((width, LANES), jnp.float32)
        second = jnp.zeros((width, LANES), jnp.float32)
        for tap in range(span):
            low = RIM + tap - margin
            first = first + first_taps[tap : tap + 1] * around_first[low : low + width]
            second = second + second_taps[tap : tap + 1] * around_second[low : low + width]
        product = first * second
        first_short[pl.ds(start, width)] = first
        second_short[pl.ds(start, width)] = second
        signal[pl.ds(start, width)] = product
        return total + jnp.sum((product * swap(product)).reshape(-1, 8, LANES), axis=0)

    gain_sum = lax.fori_loop(0, slabs, shorten, jnp.zeros((8, LANES), jnp.float32))

    def put_spectrum(found, start, count, lanes):
        for index, (real_part, imaginary) in enumerate(found):
            if imaginary is None:
                imaginary = jnp.zeros_like(real_part)
            spectra[index, pl.ds(start, count), lanes] = real_part
            spectra[index, pl.ds(width + start, count), lanes] = imaginary

    def signal_spectrum(step, carry):
        start = pl.multiple_of(step * 8, 8)
        values = [signal[pl.ds(slab * width + start, 8)] for slab in range(slabs)]
        put_spectrum(real_spectrum(values), start, 8, slice(0, LANES))
        return carry

    lax.fori_loop(0, width // 8, signal_spectrum, 0)

    wait_from(1, send_filter, recv_filter)

    def filter_spectrum(step, carry):
        start = pl.multiple_of(step * 16, 16)
        values = []
        for slab in range(slabs):
            packed = wide(recv_filter[slab // 2, pl.ds((slab % 2) * width + start, 16)])
            values.append(packed + swap(packed))
        put_spectrum(real_spectrum(values), start, 16, slice(LANES, 2 * LANES))
        return carry

    lax.fori_loop(0, width // 16, filter_spectrum, 0)

    sign = jnp.where(low_lanes((width, LANES)), 1.0, -1.0).astype(jnp.float32)
    for index in range(slabs // 2 + 1):
        found = jnp.dot(forward_ref[index], spectra[index], precision=HIGHEST)
        real_part, imaginary = found[:width, :LANES], found[width:, :LANES]
        filter_real, filter_imag = found[:width, LANES:], sign * found[width:, LANES:]
        other_real, other_imag = swap(real_part), swap(imaginary)
        spectra[index, 0:width, 0:LANES] = filter_real * real_part - filter_imag * imaginary
        spectra[index, width:, 0:LANES] = filter_real * imaginary + filter_imag * real_part
        spectra[index, 0:width, LANES:] = real_part * other_real + imaginary * other_imag
        spectra[index, width:, LANES:] = sign * (real_part * other_imag - imaginary * other_real)
        spectra[index] = jnp.dot(inverse_ref[index], spectra[index], precision=HIGHEST)

    def get_spectrum(start, count, lanes):
        found = []
        for index in range(slabs // 2 + 1):
            real_part = spectra[index, pl.ds(start, count), lanes]
            imaginary = None
            if 0 < index < slabs // 2:
                imaginary = spectra[index, pl.ds(width + start, count), lanes]
            found.append((real_part, imaginary))
        return found

    def filter_back(step, carry):
        start = pl.multiple_of(step * 16, 16)
        values = real_values(get_spectrum(start, 16, slice(LANES, 2 * LANES)))
        low = low_lanes((16, LANES))
        for slab, value in enumerate(values):
            coarse = wide(value.astype(jnp.bfloat16))
            send_response[slab // 2, pl.ds((slab % 2) * width + start, 16)] = jnp.where(
                low, coarse, value - coarse
            ).astype(jnp.bfloat16)
        return carry

    lax.fori_loop(0, width // 16, filter_back, 0)
    for hop in range(1, devices):
        peer = peer_at(hop)
        copy_to(2, hop, send_response.at[peer], recv_response, me, peer).start()
    recv_response[me] = send_response[me]

    def signal_back(step, carry):
        start = pl.multiple_of(step * 8, 8)
        values = real_values(get_spectrum(start, 8, slice(0, LANES)))
        for slab, value in enumerate(values):
            place = pl.ds(slab * width + start, 8)
            back = swap(value + gain * signal[place])
            inner = pl.ds(RIM + slab * width + start, 8)
            first_rim[1, inner] = back * second_short[place]
            second_rim[1, inner] = back * first_short[place]
        return carry

    lax.fori_loop(0, width // 8, signal_back, 0)
    close_rim(first_rim.at[1])
    close_rim(second_rim.at[1])

    def grads(block, sums):
        sums = list(sums)
        for part in range(2):
            start = pl.multiple_of(block * rows + part * width, width)
            inner = pl.ds(start, width + 2 * RIM)
            for which, (rim, taps) in enumerate(((first_rim, first_taps), (second_rim, second_taps))):
                around = rim[1, inner]
                streams = rim[0, inner]
                here = around[RIM : RIM + width]
                total = jnp.zeros((width, LANES), jnp.float32)
                for tap in range(span):
                    low = RIM + margin - tap
                    total = total + taps[tap : tap + 1] * around[low : low + width]
                    low = RIM + tap - margin
                    sums[which * span + tap] = sums[which * span + tap] + jnp.sum(
                        (here * streams[low : low + width]).reshape(-1, 8, LANES), axis=0
                    )
                send_grads[block, which, part * width : (part + 1) * width] = total.astype(
                    jnp.bfloat16
                )
        return tuple(sums)

    def step_grads(hop, sums):
        peer = peer_at(hop)
        sums = grads(peer, sums)
        copy_to(3, hop, send_grads.at[peer], recv_grads, me, peer).start()
        return sums

    sums = tuple(jnp.zeros((8, LANES), jnp.float32) for _ in range(2 * span))
    sums = lax.fori_loop(1, devices, step_grads, sums)
    sums = grads(me, sums)
    for index, value in enumerate(sums + (gain_sum,)):
        send_sums[index : index + 1] = factor * jnp.sum(value, axis=0, keepdims=True)
    for hop in range(1, devices):
        copy_to(4, hop, send_sums, recv_sums, me, peer_at(hop)).start()
    recv_sums[me] = send_sums[...]
    recv_grads[me] = send_grads[me]

    def split(first, second):
        low = low_lanes(first.shape)
        return jnp.where(low, first, swap(second)), jnp.where(low, swap(first), second)

    wait_from(2, send_response, recv_response)
    for tile in range(tiles):
        lanes = slice(tile * LANES, (tile + 1) * LANES)
        first, second = wide(recv_response[2 * tile]), wide(recv_response[2 * tile + 1])
        filter_grad_ref[:, lanes] = jnp.where(
            low_lanes(first.shape), first + swap(first), second + swap(second)
        )
    wait_from(3, send_grads, recv_grads)
    for tile in range(tiles):
        lanes = slice(tile * LANES, (tile + 1) * LANES)
        for which, targets in enumerate(
            ((streams_ref.at[1], streams_ref.at[0]), (streams_ref.at[2], output_ref))
        ):
            pieces = split(wide(recv_grads[2 * tile, which]), wide(recv_grads[2 * tile + 1, which]))
            for target, piece in zip(targets, pieces):
                target[:, lanes] = piece.astype(jnp.bfloat16)
    for hop in range(1, devices):
        copy_to(4, hop, send_sums, recv_sums, source_at(hop), peer_at(hop)).wait()
    for tile in range(tiles):
        lanes = slice(tile * LANES, (tile + 1) * LANES)
        low_part, high_part = split(recv_sums[2 * tile], recv_sums[2 * tile + 1])
        taps_grad_ref[1, :, lanes] = low_part[0:span]
        taps_grad_ref[0, :, lanes] = high_part[0:span]
        taps_grad_ref[2, :, lanes] = low_part[span : 2 * span]
        gain_grad_ref[:, lanes] = low_part[2 * span : 2 * span + 1]


def packed_body(devices, projected, long_filter, short_kernel, skip_gain, cotangent):
    rows, channels = long_filter.shape
    span = short_kernel.shape[1]
    extent = rows * devices
    slabs = 2 * devices
    tables = fine_tables(slabs, rows // 2)
    sums_rows = -(-(2 * span + 1) // 8) * 8
    block = (devices, rows, LANES)
    pair = (devices, 2, rows, LANES)
    narrow, full = jnp.bfloat16, jnp.float32
    in_vmem = pl.BlockSpec(memory_space=pltpu.VMEM)
    found = pl.pallas_call(
        functools.partial(layer_kernel, devices),
        out_shape=(
            jax.ShapeDtypeStruct((rows, channels), narrow),
            jax.ShapeDtypeStruct((3, rows, channels), narrow),
            jax.ShapeDtypeStruct((rows, channels), full),
            jax.ShapeDtypeStruct(short_kernel.shape, full),
            jax.ShapeDtypeStruct((1, channels), full),
        ),
        in_specs=[in_vmem] * 7,
        out_specs=(in_vmem,) * 5,
        scratch_shapes=[
            pltpu.VMEM(pair, narrow),
            pltpu.VMEM(pair, narrow),
            pltpu.VMEM(block, narrow),
            pltpu.VMEM(block, narrow),
            pltpu.VMEM(pair, narrow),
            pltpu.VMEM(pair, narrow),
            pltpu.VMEM(block, narrow),
            pltpu.VMEM(block, narrow),
            pltpu.VMEM((sums_rows, LANES), full),
            pltpu.VMEM((devices, sums_rows, LANES), full),
            pltpu.VMEM((2, extent + 2 * RIM, LANES), full),
            pltpu.VMEM((2, extent + 2 * RIM, LANES), full),
            pltpu.VMEM((extent, LANES), full),
            pltpu.VMEM((extent, LANES), full),
            pltpu.VMEM((extent, LANES), full),
            pltpu.VMEM((slabs // 2 + 1, rows, 2 * LANES), full),
            pltpu.SemaphoreType.DMA((5, devices)),
            pltpu.SemaphoreType.DMA((5, devices)),
        ],
        compiler_params=pltpu.CompilerParams(
            collective_id=0, has_side_effects=True, vmem_limit_bytes=40 * 1024 * 1024
        ),
    )(projected, long_filter, short_kernel, skip_gain[None], cotangent, *tables)
    return (*found[:4], found[4][0])


def with_halo(block, sides, width):
    for axis, dim in sides:
        count = lax.axis_size(axis)
        forward = [(i, i + 1) for i in range(count - 1)]
        forward.append((count - 1, 0))
        backward = [(target, source) for source, target in forward]
        low = lax.ppermute(
            lax.slice_in_dim(block, block.shape[dim] - width, None, axis=dim), axis, forward
        )
        high = lax.ppermute(lax.slice_in_dim(block, 0, width, axis=dim), axis, backward)
        block = jnp.concatenate([low, block, high], axis=dim)
    return block


def dft_tables(extent):
    indices = jnp.arange(extent, dtype=jnp.int32)
    angles = (indices[:, None] * indices[None, :] % extent).astype(jnp.float32) * (
        2.0 * math.pi / extent
    )
    return (jnp.cos(angles), jnp.sin(angles))


def apply_along(matrix, signal, axis_dim):
    letters = "wxyz"
    target = letters[:axis_dim] + "k" + letters[axis_dim + 1 :]
    return jnp.einsum(
        "k" + letters[axis_dim] + "," + letters + "->" + target, matrix, signal, precision=HIGHEST
    )


def forward_section(real_part, imaginary, axis_dim):
    cosine, sine_table = dft_tables(real_part.shape[axis_dim])
    out_real = apply_along(cosine, real_part, axis_dim)
    out_imag = -apply_along(sine_table, real_part, axis_dim)
    if imaginary is not None:
        out_real = out_real + apply_along(sine_table, imaginary, axis_dim)
        out_imag = out_imag + apply_along(cosine, imaginary, axis_dim)
    return (out_real, out_imag)


def inverse_section(real_part, imaginary, axis_dim, keep_imag):
    cosine, sine_table = dft_tables(real_part.shape[axis_dim])
    out_real = apply_along(cosine, real_part, axis_dim) - apply_along(
        sine_table, imaginary, axis_dim
    )
    if keep_imag:
        return (
            out_real,
            apply_along(sine_table, real_part, axis_dim) + apply_along(cosine, imaginary, axis_dim),
        )
    return (out_real, None)


def twist(real_part, imaginary, angles, sign_factor):
    cosine = jnp.cos(angles)
    sine_table = jnp.sin(angles)
    return (
        real_part * cosine + sign_factor * imaginary * sine_table,
        imaginary * cosine - sign_factor * real_part * sine_table,
    )


def twiddle(low_index, high_index, extent):
    return (low_index * high_index % extent).astype(jnp.float32) * (2.0 * math.pi / extent)


def block_angles(devices, portion, extent):
    low_index = jnp.arange(devices, dtype=jnp.int32)[None, :, None, None]
    high_index = (lax.axis_index("seq") * portion + jnp.arange(portion, dtype=jnp.int32))[
        None, None, :, None
    ]
    return twiddle(low_index, high_index, extent)


def sequence_forward(signals, extent):
    devices = lax.axis_size("seq")
    portion = signals.shape[1] // devices
    columns = lax.all_to_all(signals[:, None], "seq", split_axis=2, concat_axis=1, tiled=True)
    real_part, imaginary = forward_section(columns, None, 1)
    real_part, imaginary = twist(real_part, imaginary, block_angles(devices, portion, extent), 1.0)
    spread = (
        lax.all_to_all(real_part, "seq", split_axis=1, concat_axis=2, tiled=True),
        lax.all_to_all(imaginary, "seq", split_axis=1, concat_axis=2, tiled=True),
    )
    return forward_section(spread[0], spread[1], 2)


def sequence_inverse(real_part, imaginary, extent):
    devices = lax.axis_size("seq")
    portion = real_part.shape[2] // devices
    real_part, imaginary = inverse_section(real_part, imaginary, 2, True)
    gathered = (
        lax.all_to_all(real_part, "seq", split_axis=2, concat_axis=1, tiled=True),
        lax.all_to_all(imaginary, "seq", split_axis=2, concat_axis=1, tiled=True),
    )
    real_part, imaginary = twist(
        gathered[0], gathered[1], block_angles(devices, portion, extent), -1.0
    )
    pieces = inverse_section(real_part, imaginary, 1, False)[0] * (1.0 / extent)
    blocks = lax.all_to_all(pieces, "seq", split_axis=1, concat_axis=2, tiled=True)
    return blocks[:, 0]


def body(projected, long_filter, short_kernel, skip_gain, cotangent):
    rows_here = projected.shape[1]
    extent = rows_here * lax.axis_size("seq")
    factor = 1.0 / math.sqrt(extent)
    kernel_span = short_kernel.shape[1]
    margin = kernel_span // 2
    padded = with_halo(projected, (("seq", 1),), margin)
    shorts = jnp.zeros(projected.shape, jnp.float32)
    for offset in range(kernel_span):
        shorts = shorts + short_kernel[:, offset][:, None, :] * padded[
            :, offset : offset + rows_here
        ].astype(jnp.float32)
    gated_signal = shorts[1] * shorts[2]
    transform, restore = (sequence_forward, sequence_inverse)
    upstream = cotangent.astype(jnp.float32)
    grad_response = upstream * shorts[0]
    spec_real, spec_imag = transform(jnp.stack([gated_signal, long_filter]), extent)
    gated_real, gated_imag = (spec_real[0], spec_imag[0])
    filter_real, filter_imag = (spec_real[1] * factor, spec_imag[1] * factor)
    product_real = filter_real * gated_real - filter_imag * gated_imag
    product_imag = filter_real * gated_imag + filter_imag * gated_real
    convolved = restore(product_real[None], product_imag[None], extent)[0]
    upstream_real, upstream_imag = transform(grad_response[None], extent)
    upstream_real, upstream_imag = (upstream_real[0], upstream_imag[0])
    back_real = jnp.stack(
        [
            filter_real * upstream_real + filter_imag * upstream_imag,
            gated_real * upstream_real + gated_imag * upstream_imag,
        ]
    )
    back_imag = jnp.stack(
        [
            filter_real * upstream_imag - filter_imag * upstream_real,
            gated_real * upstream_imag - gated_imag * upstream_real,
        ]
    )
    restored = restore(back_real, back_imag, extent)
    grad_gated = restored[0] + skip_gain * grad_response
    filter_grad = restored[1] * factor
    response = convolved + skip_gain * gated_signal
    layer_output = (response * shorts[0]).astype(jnp.bfloat16)
    grad_shorts = jnp.stack([upstream * response, grad_gated * shorts[2], grad_gated * shorts[1]])
    rimmed = with_halo(grad_shorts, (("seq", 1),), margin)
    stream_sum = jnp.zeros(grad_shorts.shape, jnp.float32)
    kernel_terms = []
    for offset in range(kernel_span):
        start_row = 2 * margin - offset
        stream_sum = (
            stream_sum
            + short_kernel[:, offset][:, None, :] * rimmed[:, start_row : start_row + rows_here]
        )
        kernel_terms.append(
            jnp.sum(
                grad_shorts * padded[:, offset : offset + rows_here].astype(jnp.float32), axis=1
            )
        )
    kernel_part = jnp.stack(kernel_terms, axis=1)
    skip_part = jnp.sum(grad_response * gated_signal, axis=0)
    kernel_total, skip_total = lax.psum((kernel_part, skip_part), "seq")
    return (
        layer_output,
        stream_sum.astype(jnp.bfloat16),
        filter_grad,
        kernel_total * factor,
        skip_total * factor,
    )


def solution(mesh):
    placed = (
        P(None, ("groups", "seq"), "chan"),
        P(("groups", "seq"), "chan"),
        P(None, None, "chan"),
        P("chan"),
        P(("groups", "seq"), "chan"),
    )
    devices = mesh.shape["seq"]

    def run(projected, *others):
        rows, channels = projected.shape[1:]
        if channels == HALF * devices and rows == LANES and devices & (devices - 1) == 0:
            return packed_body(devices, projected, *others)
        return body(projected, *others)

    return jax.shard_map(
        run,
        mesh=mesh,
        in_specs=placed,
        out_specs=(
            P(("groups", "seq"), "chan"),
            P(None, ("groups", "seq"), "chan"),
            P(("groups", "seq"), "chan"),
            P("groups", None, "chan"),
            P(("groups", "chan")),
        ),
        check_vma=False,
    )
```

```python
import functools
import math

import jax
import jax.numpy as jnp
import numpy as np
from jax import lax
from jax.experimental import pallas as pl
from jax.experimental.pallas import tpu as pltpu
from jax.sharding import PartitionSpec as P

HIGHEST = lax.Precision.HIGHEST
LANES = 128
HALF = LANES // 2
RIM = 8
LIMIT = 64 * 1024 * 1024 - 1024 * 1024


def turned(value, step, extent):
    real_part, imaginary = value
    step = step % extent
    if step == 0:
        return value
    if 2 * step == extent:
        return (-real_part, None if imaginary is None else -imaginary)
    if 4 * step == extent:
        return (None if imaginary is None else -imaginary, real_part)
    if 4 * step == 3 * extent:
        return (imaginary, -real_part)
    cosine = math.cos(2.0 * math.pi * step / extent)
    sine = math.sin(2.0 * math.pi * step / extent)
    if imaginary is None:
        return (real_part * cosine, real_part * sine)
    return (real_part * cosine - imaginary * sine, imaginary * cosine + real_part * sine)


def part_sum(left, right, sign):
    if right is None:
        return left
    if left is None:
        return right if sign > 0 else -right
    return left + right if sign > 0 else left - right


def real_spectrum(values):
    extent = len(values)
    if extent == 2:
        return [(values[0] + values[1], None), (values[0] - values[1], None)]
    even, odd = real_spectrum(values[0::2]), real_spectrum(values[1::2])
    half = extent // 2

    def entry(spectrum, index):
        index = index % half
        if 2 * index <= half:
            return spectrum[index]
        real_part, imaginary = spectrum[half - index]
        return (real_part, None if imaginary is None else -imaginary)

    found = []
    for index in range(half + 1):
        left, right = entry(even, index), turned(entry(odd, index), -index, extent)
        found.append((part_sum(left[0], right[0], 1), part_sum(left[1], right[1], 1)))
    return found


def real_values(spectrum):
    extent = 2 * (len(spectrum) - 1)
    if extent == 2:
        first, last = spectrum[0][0], spectrum[1][0]
        return [first + last, first - last]
    half = extent // 2
    even, odd = [], []
    for index in range(half // 2 + 1):
        real_part, imaginary = spectrum[index]
        if 2 * index == half:
            even.append((2.0 * real_part, None))
            odd.append((-2.0 * imaginary, None))
            continue
        other_real, other_imag = spectrum[half - index]
        even.append(
            (real_part + other_real, part_sum(imaginary, other_imag, -1))
        )
        odd.append(
            turned(
                (real_part - other_real, part_sum(imaginary, other_imag, 1)), index, extent
            )
        )
    found = [None] * extent
    found[0::2] = real_values(even)
    found[1::2] = real_values(odd)
    return found


def fine_tables(slabs, width):
    extent = slabs * width
    coarse = np.arange(slabs // 2 + 1)[:, None, None]
    fine = np.arange(width)[None, :, None]
    place = np.arange(width)[None, None, :]
    angles = ((coarse + slabs * fine) * place % extent) * (2.0 * np.pi / extent)
    cosine, sine = np.cos(angles), np.sin(angles)
    table = np.concatenate(
        [np.concatenate([cosine, sine], 2), np.concatenate([-sine, cosine], 2)], 1
    )
    inverse = np.swapaxes(table, 1, 2) / (extent * math.sqrt(extent))
    return table.astype(np.float32), inverse.astype(np.float32)


def layer_kernel(
    devices,
    projected_in,
    cotangent_in,
    filter_in,
    taps_in,
    gain_in,
    forward_in,
    inverse_in,
    output_ref,
    streams_ref,
    filter_grad_ref,
    taps_grad_ref,
    gain_grad_ref,
    projected_ref,
    cotangent_ref,
    filter_ref,
    taps_ref,
    gain_ref,
    forward_ref,
    inverse_ref,
    send_pairs,
    recv_pairs,
    send_filter,
    recv_filter,
    send_grads,
    recv_grads,
    send_response,
    recv_response,
    send_sums,
    recv_sums,
    first_rim,
    second_rim,
    first_short,
    second_short,
    signal,
    signal_spectra,
    product_spectra,
    filter_spectra,
    load_sem,
    send_sem,
    recv_sem,
):
    arguments = (projected_in, cotangent_in, filter_in, taps_in, gain_in, forward_in, inverse_in)
    held = (
        projected_ref,
        cotangent_ref,
        filter_ref,
        taps_ref,
        gain_ref,
        forward_ref,
        inverse_ref,
    )
    loads = [
        pltpu.make_async_copy(source, target, load_sem.at[index])
        for index, (source, target) in enumerate(zip(arguments, held))
    ]
    for load in loads:
        load.start()
    rows = projected_ref.shape[1]
    span = taps_ref.shape[1]
    margin = span // 2
    width = rows // 2
    slabs = 2 * devices
    extent = rows * devices
    factor = 1.0 / math.sqrt(extent)
    tiles = devices // 2
    me = lax.axis_index("seq")
    odd = lax.rem(me, 2) == 1

    def low_lanes(shape):
        return lax.broadcasted_iota(jnp.int32, shape, 1) < HALF

    def swap(value):
        return pltpu.roll(value, HALF, 1)

    def join(first, second, parity):
        low = low_lanes(first.shape)
        if parity == 0:
            return jnp.where(low, first, swap(second))
        return jnp.where(low, swap(first), second)

    def wide(value):
        return value.astype(jnp.float32)

    def copy_to(kind, hop, source, target, slot, peer):
        return pltpu.make_async_remote_copy(
            src_ref=source,
            dst_ref=target.at[slot],
            send_sem=send_sem.at[kind, hop],
            recv_sem=recv_sem.at[kind, hop],
            device_id={"seq": peer},
            device_id_type=pl.DeviceIdType.MESH,
        )

    def peer_at(hop):
        return lax.rem(me + hop, devices)

    def source_at(hop):
        return lax.rem(me + devices - hop, devices)

    barrier = pltpu.get_barrier_semaphore()
    for hop in range(1, devices):
        pl.semaphore_signal(
            barrier, inc=1, device_id={"seq": peer_at(hop)}, device_id_type=pl.DeviceIdType.MESH
        )

    loads[0].wait()
    loads[1].wait()
    for tile in range(tiles):
        lanes = slice(tile * LANES, (tile + 1) * LANES)
        gate, left, right = [wide(projected_ref[s, :, lanes]) for s in range(3)]
        upstream = wide(cotangent_ref[:, lanes])
        for parity in range(2):
            send_pairs[2 * tile + parity, 0] = join(left, gate, parity).astype(jnp.bfloat16)
            send_pairs[2 * tile + parity, 1] = join(right, upstream, parity).astype(jnp.bfloat16)
    pl.semaphore_wait(barrier, devices - 1)
    for hop in range(1, devices):
        peer = peer_at(hop)
        copy_to(0, hop, send_pairs.at[peer], recv_pairs, me, peer).start()
    loads[2].wait()
    for tile in range(tiles):
        lanes = slice(tile * LANES, (tile + 1) * LANES)
        whole = filter_ref[:, lanes]
        coarse = wide(whole.astype(jnp.bfloat16))
        for parity in range(2):
            send_filter[2 * tile + parity] = join(coarse, whole - coarse, parity).astype(
                jnp.bfloat16
            )
    for hop in range(1, devices):
        peer = peer_at(hop)
        copy_to(1, hop, send_filter.at[peer], recv_filter, me, peer).start()
    recv_pairs[me] = send_pairs[me]
    recv_filter[me] = send_filter[me]

    for load in loads[3:5]:
        load.wait()
    own = pl.ds(pl.multiple_of((me // 2) * LANES, LANES), LANES)

    def own_pair(first, second):
        return jnp.where(odd, join(first, second, 1), join(first, second, 0))

    gate_taps, left_taps, right_taps = [taps_ref[s, :, own] for s in range(3)]
    first_taps = own_pair(left_taps, gate_taps)
    centre = wide(lax.broadcasted_iota(jnp.int32, (span, LANES), 0) == margin)
    second_taps = jnp.where(
        low_lanes((span, LANES)), own_pair(right_taps, right_taps), centre
    )
    own_gain = gain_ref[:, own]
    gain = own_pair(own_gain, own_gain)

    def wait_from(kind, source, target):
        for hop in range(1, devices):
            copy_to(kind, hop, source.at[peer_at(hop)], target, source_at(hop), peer_at(hop)).wait()

    def close_rim(rim):
        rim[0:RIM] = rim[extent : extent + RIM]
        rim[extent + RIM : extent + 2 * RIM] = rim[RIM : 2 * RIM]

    wait_from(0, send_pairs, recv_pairs)
    for block in range(devices):
        here = slice(RIM + block * rows, RIM + (block + 1) * rows)
        first_rim[0, here] = wide(recv_pairs[block, 0])
        second_rim[0, here] = wide(recv_pairs[block, 1])
    close_rim(first_rim.at[0])
    close_rim(second_rim.at[0])

    def shorten(slab, total):
        start = pl.multiple_of(slab * width, width)
        around_first = first_rim[0, pl.ds(start, width + 2 * RIM)]
        around_second = second_rim[0, pl.ds(start, width + 2 * RIM)]
        first = jnp.zeros((width, LANES), jnp.float32)
        second = jnp.zeros((width, LANES), jnp.float32)
        for tap in range(span):
            low = RIM + tap - margin
            first = first + first_taps[tap : tap + 1] * around_first[low : low + width]
            second = second + second_taps[tap : tap + 1] * around_second[low : low + width]
        product = first * second
        first_short[pl.ds(start, width)] = first
        second_short[pl.ds(start, width)] = second
        signal[pl.ds(start, width)] = product
        return total + jnp.sum((product * swap(product)).reshape(-1, 8, LANES), axis=0)

    gain_sum = lax.fori_loop(0, slabs, shorten, jnp.zeros((8, LANES), jnp.float32))

    def put_spectrum(spectra, found, start, count):
        for index, (real_part, imaginary) in enumerate(found):
            if imaginary is None:
                imaginary = jnp.zeros_like(real_part)
            spectra[index, pl.ds(start, count)] = real_part
            spectra[index, pl.ds(width + start, count)] = imaginary

    def signal_spectrum(step, carry):
        start = pl.multiple_of(step * 8, 8)
        values = [signal[pl.ds(slab * width + start, 8)] for slab in range(slabs)]
        put_spectrum(signal_spectra, real_spectrum(values), start, 8)
        return carry

    lax.fori_loop(0, width // 8, signal_spectrum, 0)

    for load in loads[5:]:
        load.wait()
    sign = jnp.where(low_lanes((width, LANES)), 1.0, -1.0).astype(jnp.float32)
    for index in range(slabs // 2 + 1):
        found = jnp.dot(forward_ref[index], signal_spectra[index], precision=HIGHEST)
        signal_spectra[index] = found
        real_part, imaginary = found[:width], found[width:]
        other_real, other_imag = swap(real_part), swap(imaginary)
        product = jnp.concatenate(
            [
                real_part * other_real + imaginary * other_imag,
                sign * (real_part * other_imag - imaginary * other_real),
            ],
            axis=0,
        )
        product_spectra[index] = jnp.dot(inverse_ref[index], product, precision=HIGHEST)

    def get_spectrum(spectra, start, count):
        found = []
        for index in range(slabs // 2 + 1):
            imaginary = None
            if 0 < index < slabs // 2:
                imaginary = spectra[index, pl.ds(width + start, count)]
            found.append((spectra[index, pl.ds(start, count)], imaginary))
        return found

    def filter_back(step, carry):
        start = pl.multiple_of(step * 16, 16)
        values = real_values(get_spectrum(product_spectra, start, 16))
        low = low_lanes((16, LANES))
        for slab, value in enumerate(values):
            coarse = wide(value.astype(jnp.bfloat16))
            send_response[slab // 2, pl.ds((slab % 2) * width + start, 16)] = jnp.where(
                low, coarse, value - coarse
            ).astype(jnp.bfloat16)
        return carry

    lax.fori_loop(0, width // 16, filter_back, 0)
    for hop in range(1, devices):
        peer = peer_at(hop)
        copy_to(2, hop, send_response.at[peer], recv_response, me, peer).start()
    recv_response[me] = send_response[me]

    wait_from(1, send_filter, recv_filter)

    def filter_spectrum(step, carry):
        start = pl.multiple_of(step * 16, 16)
        values = []
        for slab in range(slabs):
            packed = wide(recv_filter[slab // 2, pl.ds((slab % 2) * width + start, 16)])
            values.append(packed + swap(packed))
        put_spectrum(filter_spectra, real_spectrum(values), start, 16)
        return carry

    lax.fori_loop(0, width // 16, filter_spectrum, 0)

    for index in range(slabs // 2 + 1):
        found = jnp.dot(forward_ref[index], filter_spectra[index], precision=HIGHEST)
        filter_real, filter_imag = found[:width], sign * found[width:]
        real_part, imaginary = signal_spectra[index, :width], signal_spectra[index, width:]
        product = jnp.concatenate(
            [
                filter_real * real_part - filter_imag * imaginary,
                filter_real * imaginary + filter_imag * real_part,
            ],
            axis=0,
        )
        filter_spectra[index] = jnp.dot(inverse_ref[index], product, precision=HIGHEST)

    def signal_back(step, carry):
        start = pl.multiple_of(step * 8, 8)
        values = real_values(get_spectrum(filter_spectra, start, 8))
        for slab, value in enumerate(values):
            place = pl.ds(slab * width + start, 8)
            back = swap(value + gain * signal[place])
            inner = pl.ds(RIM + slab * width + start, 8)
            first_rim[1, inner] = back * second_short[place]
            second_rim[1, inner] = back * first_short[place]
        return carry

    lax.fori_loop(0, width // 8, signal_back, 0)
    close_rim(first_rim.at[1])
    close_rim(second_rim.at[1])

    def grads(block, sums):
        sums = list(sums)
        for part in range(2):
            start = pl.multiple_of(block * rows + part * width, width)
            inner = pl.ds(start, width + 2 * RIM)
            for which, (rim, taps) in enumerate(((first_rim, first_taps), (second_rim, second_taps))):
                around = rim[1, inner]
                streams = rim[0, inner]
                here = around[RIM : RIM + width]
                total = jnp.zeros((width, LANES), jnp.float32)
                for tap in range(span):
                    low = RIM + margin - tap
                    total = total + taps[tap : tap + 1] * around[low : low + width]
                    low = RIM + tap - margin
                    sums[which * span + tap] = sums[which * span + tap] + jnp.sum(
                        (here * streams[low : low + width]).reshape(-1, 8, LANES), axis=0
                    )
                send_grads[block, which, part * width : (part + 1) * width] = total.astype(
                    jnp.bfloat16
                )
        return tuple(sums)

    def step_grads(hop, sums):
        peer = peer_at(hop)
        sums = grads(peer, sums)
        copy_to(3, hop, send_grads.at[peer], recv_grads, me, peer).start()
        return sums

    sums = tuple(jnp.zeros((8, LANES), jnp.float32) for _ in range(2 * span))
    sums = lax.fori_loop(1, devices, step_grads, sums)
    sums = grads(me, sums)
    for index, value in enumerate(sums + (gain_sum,)):
        send_sums[index : index + 1] = factor * jnp.sum(value, axis=0, keepdims=True)
    for hop in range(1, devices):
        copy_to(4, hop, send_sums, recv_sums, me, peer_at(hop)).start()
    recv_sums[me] = send_sums[...]
    recv_grads[me] = send_grads[me]

    def split(first, second):
        low = low_lanes(first.shape)
        return jnp.where(low, first, swap(second)), jnp.where(low, swap(first), second)

    wait_from(2, send_response, recv_response)
    for tile in range(tiles):
        lanes = slice(tile * LANES, (tile + 1) * LANES)
        first, second = wide(recv_response[2 * tile]), wide(recv_response[2 * tile + 1])
        filter_grad_ref[:, lanes] = jnp.where(
            low_lanes(first.shape), first + swap(first), second + swap(second)
        )
    wait_from(3, send_grads, recv_grads)
    for tile in range(tiles):
        lanes = slice(tile * LANES, (tile + 1) * LANES)
        for which, targets in enumerate(
            ((streams_ref.at[1], streams_ref.at[0]), (streams_ref.at[2], output_ref))
        ):
            pieces = split(wide(recv_grads[2 * tile, which]), wide(recv_grads[2 * tile + 1, which]))
            for target, piece in zip(targets, pieces):
                target[:, lanes] = piece.astype(jnp.bfloat16)
    for hop in range(1, devices):
        copy_to(4, hop, send_sums, recv_sums, source_at(hop), peer_at(hop)).wait()
    for tile in range(tiles):
        lanes = slice(tile * LANES, (tile + 1) * LANES)
        low_part, high_part = split(recv_sums[2 * tile], recv_sums[2 * tile + 1])
        taps_grad_ref[1, :, lanes] = low_part[0:span]
        taps_grad_ref[0, :, lanes] = high_part[0:span]
        taps_grad_ref[2, :, lanes] = low_part[span : 2 * span]
        gain_grad_ref[:, lanes] = low_part[2 * span : 2 * span + 1]


def store_kernel(*refs):
    sem = refs[10]
    copies = [pltpu.make_async_copy(refs[i], refs[5 + i], sem.at[i]) for i in range(5)]
    for copy in copies:
        copy.start()
    for copy in copies:
        copy.wait()


def packed_body(devices, projected, long_filter, short_kernel, skip_gain, cotangent):
    rows, channels = long_filter.shape
    span = short_kernel.shape[1]
    extent = rows * devices
    slabs = 2 * devices
    tables = fine_tables(slabs, rows // 2)
    sums_rows = -(-(2 * span + 1) // 8) * 8
    block = (devices, rows, LANES)
    pair = (devices, 2, rows, LANES)
    narrow, full = jnp.bfloat16, jnp.float32
    arguments = (projected, cotangent, long_filter, short_kernel, skip_gain[None], *tables)
    in_vmem = pl.BlockSpec(memory_space=pltpu.VMEM)
    found = pl.pallas_call(
        functools.partial(layer_kernel, devices),
        out_shape=(
            jax.ShapeDtypeStruct((rows, channels), narrow),
            jax.ShapeDtypeStruct((3, rows, channels), narrow),
            jax.ShapeDtypeStruct((rows, channels), full),
            jax.ShapeDtypeStruct(short_kernel.shape, full),
            jax.ShapeDtypeStruct((1, channels), full),
        ),
        in_specs=[pl.BlockSpec(memory_space=pltpu.HBM)] * 7,
        out_specs=(in_vmem,) * 5,
        scratch_shapes=[
            *(pltpu.VMEM(value.shape, value.dtype) for value in arguments),
            pltpu.VMEM(pair, narrow),
            pltpu.VMEM(pair, narrow),
            pltpu.VMEM(block, narrow),
            pltpu.VMEM(block, narrow),
            pltpu.VMEM(pair, narrow),
            pltpu.VMEM(pair, narrow),
            pltpu.VMEM(block, narrow),
            pltpu.VMEM(block, narrow),
            pltpu.VMEM((sums_rows, LANES), full),
            pltpu.VMEM((devices, sums_rows, LANES), full),
            pltpu.VMEM((2, extent + 2 * RIM, LANES), full),
            pltpu.VMEM((2, extent + 2 * RIM, LANES), full),
            pltpu.VMEM((extent, LANES), full),
            pltpu.VMEM((extent, LANES), full),
            pltpu.VMEM((extent, LANES), full),
            *[pltpu.VMEM((slabs // 2 + 1, rows, LANES), full)] * 3,
            pltpu.SemaphoreType.DMA((len(arguments),)),
            pltpu.SemaphoreType.DMA((5, devices)),
            pltpu.SemaphoreType.DMA((5, devices)),
        ],
        compiler_params=pltpu.CompilerParams(
            collective_id=0, has_side_effects=True, vmem_limit_bytes=LIMIT
        ),
    )(*arguments)
    found = pl.pallas_call(
        store_kernel,
        out_shape=tuple(jax.ShapeDtypeStruct(value.shape, value.dtype) for value in found),
        in_specs=[in_vmem] * 5,
        out_specs=(pl.BlockSpec(memory_space=pltpu.HBM),) * 5,
        scratch_shapes=[pltpu.SemaphoreType.DMA((5,))],
        compiler_params=pltpu.CompilerParams(vmem_limit_bytes=LIMIT),
    )(*found)
    return (*found[:4], found[4][0])


def with_halo(block, sides, width):
    for axis, dim in sides:
        count = lax.axis_size(axis)
        forward = [(i, i + 1) for i in range(count - 1)]
        forward.append((count - 1, 0))
        backward = [(target, source) for source, target in forward]
        low = lax.ppermute(
            lax.slice_in_dim(block, block.shape[dim] - width, None, axis=dim), axis, forward
        )
        high = lax.ppermute(lax.slice_in_dim(block, 0, width, axis=dim), axis, backward)
        block = jnp.concatenate([low, block, high], axis=dim)
    return block


def dft_tables(extent):
    indices = jnp.arange(extent, dtype=jnp.int32)
    angles = (indices[:, None] * indices[None, :] % extent).astype(jnp.float32) * (
        2.0 * math.pi / extent
    )
    return (jnp.cos(angles), jnp.sin(angles))


def apply_along(matrix, signal, axis_dim):
    letters = "wxyz"
    target = letters[:axis_dim] + "k" + letters[axis_dim + 1 :]
    return jnp.einsum(
        "k" + letters[axis_dim] + "," + letters + "->" + target, matrix, signal, precision=HIGHEST
    )


def forward_section(real_part, imaginary, axis_dim):
    cosine, sine_table = dft_tables(real_part.shape[axis_dim])
    out_real = apply_along(cosine, real_part, axis_dim)
    out_imag = -apply_along(sine_table, real_part, axis_dim)
    if imaginary is not None:
        out_real = out_real + apply_along(sine_table, imaginary, axis_dim)
        out_imag = out_imag + apply_along(cosine, imaginary, axis_dim)
    return (out_real, out_imag)


def inverse_section(real_part, imaginary, axis_dim, keep_imag):
    cosine, sine_table = dft_tables(real_part.shape[axis_dim])
    out_real = apply_along(cosine, real_part, axis_dim) - apply_along(
        sine_table, imaginary, axis_dim
    )
    if keep_imag:
        return (
            out_real,
            apply_along(sine_table, real_part, axis_dim) + apply_along(cosine, imaginary, axis_dim),
        )
    return (out_real, None)


def twist(real_part, imaginary, angles, sign_factor):
    cosine = jnp.cos(angles)
    sine_table = jnp.sin(angles)
    return (
        real_part * cosine + sign_factor * imaginary * sine_table,
        imaginary * cosine - sign_factor * real_part * sine_table,
    )


def twiddle(low_index, high_index, extent):
    return (low_index * high_index % extent).astype(jnp.float32) * (2.0 * math.pi / extent)


def block_angles(devices, portion, extent):
    low_index = jnp.arange(devices, dtype=jnp.int32)[None, :, None, None]
    high_index = (lax.axis_index("seq") * portion + jnp.arange(portion, dtype=jnp.int32))[
        None, None, :, None
    ]
    return twiddle(low_index, high_index, extent)


def sequence_forward(signals, extent):
    devices = lax.axis_size("seq")
    portion = signals.shape[1] // devices
    columns = lax.all_to_all(signals[:, None], "seq", split_axis=2, concat_axis=1, tiled=True)
    real_part, imaginary = forward_section(columns, None, 1)
    real_part, imaginary = twist(real_part, imaginary, block_angles(devices, portion, extent), 1.0)
    spread = (
        lax.all_to_all(real_part, "seq", split_axis=1, concat_axis=2, tiled=True),
        lax.all_to_all(imaginary, "seq", split_axis=1, concat_axis=2, tiled=True),
    )
    return forward_section(spread[0], spread[1], 2)


def sequence_inverse(real_part, imaginary, extent):
    devices = lax.axis_size("seq")
    portion = real_part.shape[2] // devices
    real_part, imaginary = inverse_section(real_part, imaginary, 2, True)
    gathered = (
        lax.all_to_all(real_part, "seq", split_axis=2, concat_axis=1, tiled=True),
        lax.all_to_all(imaginary, "seq", split_axis=2, concat_axis=1, tiled=True),
    )
    real_part, imaginary = twist(
        gathered[0], gathered[1], block_angles(devices, portion, extent), -1.0
    )
    pieces = inverse_section(real_part, imaginary, 1, False)[0] * (1.0 / extent)
    blocks = lax.all_to_all(pieces, "seq", split_axis=1, concat_axis=2, tiled=True)
    return blocks[:, 0]


def body(projected, long_filter, short_kernel, skip_gain, cotangent):
    rows_here = projected.shape[1]
    extent = rows_here * lax.axis_size("seq")
    factor = 1.0 / math.sqrt(extent)
    kernel_span = short_kernel.shape[1]
    margin = kernel_span // 2
    padded = with_halo(projected, (("seq", 1),), margin)
    shorts = jnp.zeros(projected.shape, jnp.float32)
    for offset in range(kernel_span):
        shorts = shorts + short_kernel[:, offset][:, None, :] * padded[
            :, offset : offset + rows_here
        ].astype(jnp.float32)
    gated_signal = shorts[1] * shorts[2]
    transform, restore = (sequence_forward, sequence_inverse)
    upstream = cotangent.astype(jnp.float32)
    grad_response = upstream * shorts[0]
    spec_real, spec_imag = transform(jnp.stack([gated_signal, long_filter]), extent)
    gated_real, gated_imag = (spec_real[0], spec_imag[0])
    filter_real, filter_imag = (spec_real[1] * factor, spec_imag[1] * factor)
    product_real = filter_real * gated_real - filter_imag * gated_imag
    product_imag = filter_real * gated_imag + filter_imag * gated_real
    convolved = restore(product_real[None], product_imag[None], extent)[0]
    upstream_real, upstream_imag = transform(grad_response[None], extent)
    upstream_real, upstream_imag = (upstream_real[0], upstream_imag[0])
    back_real = jnp.stack(
        [
            filter_real * upstream_real + filter_imag * upstream_imag,
            gated_real * upstream_real + gated_imag * upstream_imag,
        ]
    )
    back_imag = jnp.stack(
        [
            filter_real * upstream_imag - filter_imag * upstream_real,
            gated_real * upstream_imag - gated_imag * upstream_real,
        ]
    )
    restored = restore(back_real, back_imag, extent)
    grad_gated = restored[0] + skip_gain * grad_response
    filter_grad = restored[1] * factor
    response = convolved + skip_gain * gated_signal
    layer_output = (response * shorts[0]).astype(jnp.bfloat16)
    grad_shorts = jnp.stack([upstream * response, grad_gated * shorts[2], grad_gated * shorts[1]])
    rimmed = with_halo(grad_shorts, (("seq", 1),), margin)
    stream_sum = jnp.zeros(grad_shorts.shape, jnp.float32)
    kernel_terms = []
    for offset in range(kernel_span):
        start_row = 2 * margin - offset
        stream_sum = (
            stream_sum
            + short_kernel[:, offset][:, None, :] * rimmed[:, start_row : start_row + rows_here]
        )
        kernel_terms.append(
            jnp.sum(
                grad_shorts * padded[:, offset : offset + rows_here].astype(jnp.float32), axis=1
            )
        )
    kernel_part = jnp.stack(kernel_terms, axis=1)
    skip_part = jnp.sum(grad_response * gated_signal, axis=0)
    kernel_total, skip_total = lax.psum((kernel_part, skip_part), "seq")
    return (
        layer_output,
        stream_sum.astype(jnp.bfloat16),
        filter_grad,
        kernel_total * factor,
        skip_total * factor,
    )


def solution(mesh):
    placed = (
        P(None, ("groups", "seq"), "chan"),
        P(("groups", "seq"), "chan"),
        P(None, None, "chan"),
        P("chan"),
        P(("groups", "seq"), "chan"),
    )
    devices = mesh.shape["seq"]

    def run(projected, *others):
        rows, channels = projected.shape[1:]
        if channels == HALF * devices and rows == LANES and devices & (devices - 1) == 0:
            return packed_body(devices, projected, *others)
        return body(projected, *others)

    return jax.shard_map(
        run,
        mesh=mesh,
        in_specs=placed,
        out_specs=(
            P(("groups", "seq"), "chan"),
            P(None, ("groups", "seq"), "chan"),
            P(("groups", "seq"), "chan"),
            P("groups", None, "chan"),
            P(("groups", "chan")),
        ),
        check_vma=False,
    )
```

```python
import functools
import math

import jax
import jax.numpy as jnp
import numpy as np
from jax import lax
from jax.experimental import pallas as pl
from jax.experimental.pallas import tpu as pltpu
from jax.sharding import PartitionSpec as P

HIGHEST = lax.Precision.HIGHEST
LANES = 128
HALF = LANES // 2
RIM = 8
LIMIT = 64 * 1024 * 1024 - 1024 * 1024


def turned(value, step, extent):
    real_part, imaginary = value
    step = step % extent
    if step == 0:
        return value
    if 2 * step == extent:
        return (-real_part, None if imaginary is None else -imaginary)
    if 4 * step == extent:
        return (None if imaginary is None else -imaginary, real_part)
    if 4 * step == 3 * extent:
        return (imaginary, -real_part)
    cosine = math.cos(2.0 * math.pi * step / extent)
    sine = math.sin(2.0 * math.pi * step / extent)
    if imaginary is None:
        return (real_part * cosine, real_part * sine)
    return (real_part * cosine - imaginary * sine, imaginary * cosine + real_part * sine)


def part_sum(left, right, sign):
    if right is None:
        return left
    if left is None:
        return right if sign > 0 else -right
    return left + right if sign > 0 else left - right


def real_spectrum(values):
    extent = len(values)
    if extent == 2:
        return [(values[0] + values[1], None), (values[0] - values[1], None)]
    even, odd = real_spectrum(values[0::2]), real_spectrum(values[1::2])
    half = extent // 2

    def entry(spectrum, index):
        index = index % half
        if 2 * index <= half:
            return spectrum[index]
        real_part, imaginary = spectrum[half - index]
        return (real_part, None if imaginary is None else -imaginary)

    found = []
    for index in range(half + 1):
        left, right = entry(even, index), turned(entry(odd, index), -index, extent)
        found.append((part_sum(left[0], right[0], 1), part_sum(left[1], right[1], 1)))
    return found


def real_values(spectrum):
    extent = 2 * (len(spectrum) - 1)
    if extent == 2:
        first, last = spectrum[0][0], spectrum[1][0]
        return [first + last, first - last]
    half = extent // 2
    even, odd = [], []
    for index in range(half // 2 + 1):
        real_part, imaginary = spectrum[index]
        if 2 * index == half:
            even.append((2.0 * real_part, None))
            odd.append((-2.0 * imaginary, None))
            continue
        other_real, other_imag = spectrum[half - index]
        even.append(
            (real_part + other_real, part_sum(imaginary, other_imag, -1))
        )
        odd.append(
            turned(
                (real_part - other_real, part_sum(imaginary, other_imag, 1)), index, extent
            )
        )
    found = [None] * extent
    found[0::2] = real_values(even)
    found[1::2] = real_values(odd)
    return found


def fine_tables(slabs, width):
    extent = slabs * width
    coarse = np.arange(slabs // 2 + 1)[:, None, None]
    fine = np.arange(width)[None, :, None]
    place = np.arange(width)[None, None, :]
    angles = ((coarse + slabs * fine) * place % extent) * (2.0 * np.pi / extent)
    cosine, sine = np.cos(angles), np.sin(angles)
    table = np.concatenate(
        [np.concatenate([cosine, sine], 2), np.concatenate([-sine, cosine], 2)], 1
    )
    inverse = np.swapaxes(table, 1, 2) / (extent * math.sqrt(extent))
    return table.astype(np.float32), inverse.astype(np.float32)


def layer_kernel(
    devices,
    projected_in,
    cotangent_in,
    filter_in,
    taps_in,
    gain_in,
    forward_in,
    inverse_in,
    recv_response,
    recv_grads,
    recv_sums,
    projected_ref,
    cotangent_ref,
    filter_ref,
    taps_ref,
    gain_ref,
    forward_ref,
    inverse_ref,
    send_pairs,
    recv_pairs,
    send_filter,
    recv_filter,
    send_grads,
    send_response,
    send_sums,
    first_rim,
    second_rim,
    first_short,
    second_short,
    signal,
    signal_spectra,
    product_spectra,
    filter_spectra,
    load_sem,
    keep_sem,
    send_sem,
    recv_sem,
):
    hops = [(devices // 2 + (-1) ** i * ((i + 1) // 2)) for i in range(devices - 1)]
    arguments = (projected_in, cotangent_in, filter_in, taps_in, gain_in, forward_in, inverse_in)
    held = (
        projected_ref,
        cotangent_ref,
        filter_ref,
        taps_ref,
        gain_ref,
        forward_ref,
        inverse_ref,
    )
    loads = [
        pltpu.make_async_copy(source, target, load_sem.at[index])
        for index, (source, target) in enumerate(zip(arguments, held))
    ]
    for load in loads:
        load.start()
    rows = projected_ref.shape[1]
    span = taps_ref.shape[1]
    margin = span // 2
    width = rows // 2
    slabs = 2 * devices
    extent = rows * devices
    factor = 1.0 / math.sqrt(extent)
    me = lax.axis_index("seq")
    odd = lax.rem(me, 2) == 1

    def low_lanes(shape):
        return lax.broadcasted_iota(jnp.int32, shape, 1) < HALF

    def swap(value):
        return pltpu.roll(value, HALF, 1)

    def join(first, second, parity):
        low = low_lanes(first.shape)
        if parity == 0:
            return jnp.where(low, first, swap(second))
        return jnp.where(low, swap(first), second)

    def wide(value):
        return value.astype(jnp.float32)

    def copy_to(kind, hop, source, target, slot, peer):
        return pltpu.make_async_remote_copy(
            src_ref=source,
            dst_ref=target.at[slot],
            send_sem=send_sem.at[kind, hop],
            recv_sem=recv_sem.at[kind, hop],
            device_id={"seq": peer},
            device_id_type=pl.DeviceIdType.MESH,
        )

    def peer_at(hop):
        return lax.rem(me + hop, devices)

    def source_at(hop):
        return lax.rem(me + devices - hop, devices)

    barrier = pltpu.get_barrier_semaphore()
    for hop in hops:
        pl.semaphore_signal(
            barrier, inc=1, device_id={"seq": peer_at(hop)}, device_id_type=pl.DeviceIdType.MESH
        )

    loads[0].wait()
    loads[1].wait()
    def lanes_of(peer):
        return pl.ds(pl.multiple_of((peer // 2) * LANES, LANES), LANES)

    def join_for(peer, first, second):
        flip = lax.rem(peer, 2) == 1
        return jnp.where(
            low_lanes(first.shape),
            jnp.where(flip, swap(first), first),
            jnp.where(flip, second, swap(second)),
        ).astype(jnp.bfloat16)

    def pack_pairs(peer, target):
        lanes = lanes_of(peer)
        gate, left, right = [wide(projected_ref[s, :, lanes]) for s in range(3)]
        target[0] = join_for(peer, left, gate)
        target[1] = join_for(peer, right, wide(cotangent_ref[:, lanes]))

    def pack_filter(peer, target):
        whole = filter_ref[:, lanes_of(peer)]
        coarse = wide(whole.astype(jnp.bfloat16))
        target[...] = join_for(peer, coarse, whole - coarse)

    for place, hop in enumerate(hops):
        peer = peer_at(hop)
        pack_pairs(peer, send_pairs.at[peer])
        if place == 0:
            pl.semaphore_wait(barrier, devices - 1)
        copy_to(0, hop, send_pairs.at[peer], recv_pairs, me, peer).start()
    loads[2].wait()
    for hop in hops:
        peer = peer_at(hop)
        pack_filter(peer, send_filter.at[peer])
        copy_to(1, hop, send_filter.at[peer], recv_filter, me, peer).start()
    pack_pairs(me, recv_pairs.at[me])
    pack_filter(me, recv_filter.at[me])

    for load in loads[3:5]:
        load.wait()
    own = pl.ds(pl.multiple_of((me // 2) * LANES, LANES), LANES)

    def own_pair(first, second):
        return jnp.where(odd, join(first, second, 1), join(first, second, 0))

    gate_taps, left_taps, right_taps = [taps_ref[s, :, own] for s in range(3)]
    first_taps = own_pair(left_taps, gate_taps)
    centre = wide(lax.broadcasted_iota(jnp.int32, (span, LANES), 0) == margin)
    second_taps = jnp.where(
        low_lanes((span, LANES)), own_pair(right_taps, right_taps), centre
    )
    own_gain = gain_ref[:, own]
    gain = own_pair(own_gain, own_gain)

    def wait_from(kind, source, target):
        for hop in hops:
            copy_to(kind, hop, source.at[peer_at(hop)], target, source_at(hop), peer_at(hop)).wait()

    def close_rim(rim):
        rim[0:RIM] = rim[extent : extent + RIM]
        rim[extent + RIM : extent + 2 * RIM] = rim[RIM : 2 * RIM]

    wait_from(0, send_pairs, recv_pairs)
    for block in range(devices):
        here = slice(RIM + block * rows, RIM + (block + 1) * rows)
        first_rim[0, here] = wide(recv_pairs[block, 0])
        second_rim[0, here] = wide(recv_pairs[block, 1])
    close_rim(first_rim.at[0])
    close_rim(second_rim.at[0])

    def shorten(slab, total):
        start = pl.multiple_of(slab * width, width)
        around_first = first_rim[0, pl.ds(start, width + 2 * RIM)]
        around_second = second_rim[0, pl.ds(start, width + 2 * RIM)]
        first = jnp.zeros((width, LANES), jnp.float32)
        second = jnp.zeros((width, LANES), jnp.float32)
        for tap in range(span):
            low = RIM + tap - margin
            first = first + first_taps[tap : tap + 1] * around_first[low : low + width]
            second = second + second_taps[tap : tap + 1] * around_second[low : low + width]
        product = first * second
        first_short[pl.ds(start, width)] = first
        second_short[pl.ds(start, width)] = second
        signal[pl.ds(start, width)] = product
        return total + jnp.sum((product * swap(product)).reshape(-1, 8, LANES), axis=0)

    gain_sum = lax.fori_loop(0, slabs, shorten, jnp.zeros((8, LANES), jnp.float32))

    def put_spectrum(spectra, found, start, count):
        for index, (real_part, imaginary) in enumerate(found):
            if imaginary is None:
                imaginary = jnp.zeros_like(real_part)
            spectra[index, pl.ds(start, count)] = real_part
            spectra[index, pl.ds(width + start, count)] = imaginary

    def signal_spectrum(step, carry):
        start = pl.multiple_of(step * 8, 8)
        values = [signal[pl.ds(slab * width + start, 8)] for slab in range(slabs)]
        put_spectrum(signal_spectra, real_spectrum(values), start, 8)
        return carry

    lax.fori_loop(0, width // 8, signal_spectrum, 0)

    for load in loads[5:]:
        load.wait()
    sign = jnp.where(low_lanes((width, LANES)), 1.0, -1.0).astype(jnp.float32)
    for index in range(slabs // 2 + 1):
        found = jnp.dot(forward_ref[index], signal_spectra[index], precision=HIGHEST)
        signal_spectra[index] = found
        real_part, imaginary = found[:width], found[width:]
        other_real, other_imag = swap(real_part), swap(imaginary)
        product = jnp.concatenate(
            [
                real_part * other_real + imaginary * other_imag,
                sign * (real_part * other_imag - imaginary * other_real),
            ],
            axis=0,
        )
        product_spectra[index] = jnp.dot(inverse_ref[index], product, precision=HIGHEST)

    def get_spectrum(spectra, start, count):
        found = []
        for index in range(slabs // 2 + 1):
            imaginary = None
            if 0 < index < slabs // 2:
                imaginary = spectra[index, pl.ds(width + start, count)]
            found.append((spectra[index, pl.ds(start, count)], imaginary))
        return found

    def filter_back(step, carry):
        start = pl.multiple_of(step * 16, 16)
        values = real_values(get_spectrum(product_spectra, start, 16))
        low = low_lanes((16, LANES))
        for slab, value in enumerate(values):
            coarse = wide(value.astype(jnp.bfloat16))
            send_response[slab // 2, pl.ds((slab % 2) * width + start, 16)] = jnp.where(
                low, coarse, value - coarse
            ).astype(jnp.bfloat16)
        return carry

    lax.fori_loop(0, width // 16, filter_back, 0)
    for hop in hops:
        peer = peer_at(hop)
        copy_to(2, hop, send_response.at[peer], recv_response, me, peer).start()
    kept = [
        pltpu.make_async_copy(source, target.at[me], keep_sem.at[index])
        for index, (source, target) in enumerate(
            (
                (send_response.at[me], recv_response),
                (send_grads.at[me], recv_grads),
                (send_sums, recv_sums),
            )
        )
    ]
    kept[0].start()

    wait_from(1, send_filter, recv_filter)

    def filter_spectrum(step, carry):
        start = pl.multiple_of(step * 16, 16)
        values = []
        for slab in range(slabs):
            packed = wide(recv_filter[slab // 2, pl.ds((slab % 2) * width + start, 16)])
            values.append(packed + swap(packed))
        put_spectrum(filter_spectra, real_spectrum(values), start, 16)
        return carry

    lax.fori_loop(0, width // 16, filter_spectrum, 0)

    for index in range(slabs // 2 + 1):
        found = jnp.dot(forward_ref[index], filter_spectra[index], precision=HIGHEST)
        filter_real, filter_imag = found[:width], sign * found[width:]
        real_part, imaginary = signal_spectra[index, :width], signal_spectra[index, width:]
        product = jnp.concatenate(
            [
                filter_real * real_part - filter_imag * imaginary,
                filter_real * imaginary + filter_imag * real_part,
            ],
            axis=0,
        )
        filter_spectra[index] = jnp.dot(inverse_ref[index], product, precision=HIGHEST)

    def signal_back(step, carry):
        start = pl.multiple_of(step * 8, 8)
        values = real_values(get_spectrum(filter_spectra, start, 8))
        for slab, value in enumerate(values):
            place = pl.ds(slab * width + start, 8)
            back = swap(value + gain * signal[place])
            inner = pl.ds(RIM + slab * width + start, 8)
            first_rim[1, inner] = back * second_short[place]
            second_rim[1, inner] = back * first_short[place]
        return carry

    lax.fori_loop(0, width // 8, signal_back, 0)
    close_rim(first_rim.at[1])
    close_rim(second_rim.at[1])

    def grads(block, sums):
        sums = list(sums)
        for part in range(2):
            start = pl.multiple_of(block * rows + part * width, width)
            inner = pl.ds(start, width + 2 * RIM)
            for which, (rim, taps) in enumerate(((first_rim, first_taps), (second_rim, second_taps))):
                around = rim[1, inner]
                streams = rim[0, inner]
                here = around[RIM : RIM + width]
                total = jnp.zeros((width, LANES), jnp.float32)
                for tap in range(span):
                    low = RIM + margin - tap
                    total = total + taps[tap : tap + 1] * around[low : low + width]
                    low = RIM + tap - margin
                    sums[which * span + tap] = sums[which * span + tap] + jnp.sum(
                        (here * streams[low : low + width]).reshape(-1, 8, LANES), axis=0
                    )
                send_grads[block, which, part * width : (part + 1) * width] = total.astype(
                    jnp.bfloat16
                )
        return tuple(sums)

    def step_grads(step, sums):
        hop = devices // 2 + (step + 1) // 2 * (1 - 2 * lax.rem(step, 2))
        peer = peer_at(hop)
        sums = grads(peer, sums)
        copy_to(3, hop, send_grads.at[peer], recv_grads, me, peer).start()
        return sums

    sums = tuple(jnp.zeros((8, LANES), jnp.float32) for _ in range(2 * span))
    sums = lax.fori_loop(0, devices - 1, step_grads, sums)
    sums = grads(me, sums)
    for index, value in enumerate(sums + (gain_sum,)):
        send_sums[index : index + 1] = factor * jnp.sum(value, axis=0, keepdims=True)
    for hop in hops:
        copy_to(4, hop, send_sums, recv_sums, me, peer_at(hop)).start()
    kept[1].start()
    kept[2].start()
    for keep in kept:
        keep.wait()
    wait_from(2, send_response, recv_response)
    wait_from(3, send_grads, recv_grads)
    for hop in hops:
        copy_to(4, hop, send_sums, recv_sums, source_at(hop), peer_at(hop)).wait()


def unpack_kernel(*refs):
    packed, results, held, refs = refs[:3], refs[3:8], refs[8:11], refs[11:]
    output_ref, streams_ref, filter_grad_ref, taps_grad_ref, gain_grad_ref = refs[:5]
    recv_response, recv_grads, recv_sums = held
    load_sem, store_sem = refs[5:]
    loads = [pltpu.make_async_copy(packed[i], held[i], load_sem.at[i]) for i in range(3)]
    stores = [pltpu.make_async_copy(refs[i], results[i], store_sem.at[i]) for i in range(5)]
    for load in loads:
        load.start()
    tiles = recv_response.shape[0] // 2
    span = taps_grad_ref.shape[1]

    def low_lanes(shape):
        return lax.broadcasted_iota(jnp.int32, shape, 1) < HALF

    def swap(value):
        return pltpu.roll(value, HALF, 1)

    def wide(value):
        return value.astype(jnp.float32)

    def split(first, second):
        low = low_lanes(first.shape)
        return jnp.where(low, first, swap(second)), jnp.where(low, swap(first), second)

    loads[0].wait()
    for tile in range(tiles):
        lanes = slice(tile * LANES, (tile + 1) * LANES)
        first, second = wide(recv_response[2 * tile]), wide(recv_response[2 * tile + 1])
        filter_grad_ref[:, lanes] = jnp.where(
            low_lanes(first.shape), first + swap(first), second + swap(second)
        )
    stores[2].start()
    loads[1].wait()
    for tile in range(tiles):
        lanes = slice(tile * LANES, (tile + 1) * LANES)
        for which, targets in enumerate(
            ((streams_ref.at[1], streams_ref.at[0]), (streams_ref.at[2], output_ref))
        ):
            pieces = split(wide(recv_grads[2 * tile, which]), wide(recv_grads[2 * tile + 1, which]))
            for target, piece in zip(targets, pieces):
                target[:, lanes] = piece.astype(jnp.bfloat16)
    stores[0].start()
    stores[1].start()
    loads[2].wait()
    for tile in range(tiles):
        lanes = slice(tile * LANES, (tile + 1) * LANES)
        low_part, high_part = split(recv_sums[2 * tile], recv_sums[2 * tile + 1])
        taps_grad_ref[1, :, lanes] = low_part[0:span]
        taps_grad_ref[0, :, lanes] = high_part[0:span]
        taps_grad_ref[2, :, lanes] = low_part[span : 2 * span]
        gain_grad_ref[:, lanes] = low_part[2 * span : 2 * span + 1]
    stores[3].start()
    stores[4].start()
    for store in stores:
        store.wait()


def packed_body(devices, projected, long_filter, short_kernel, skip_gain, cotangent):
    rows, channels = long_filter.shape
    span = short_kernel.shape[1]
    extent = rows * devices
    slabs = 2 * devices
    tables = fine_tables(slabs, rows // 2)
    sums_rows = -(-(2 * span + 1) // 8) * 8
    block = (devices, rows, LANES)
    pair = (devices, 2, rows, LANES)
    narrow, full = jnp.bfloat16, jnp.float32
    arguments = (projected, cotangent, long_filter, short_kernel, skip_gain[None], *tables)
    in_hbm = pl.BlockSpec(memory_space=pltpu.HBM)
    packed_shapes = (
        jax.ShapeDtypeStruct(block, narrow),
        jax.ShapeDtypeStruct(pair, narrow),
        jax.ShapeDtypeStruct((devices, sums_rows, LANES), full),
    )
    out_shapes = (
        jax.ShapeDtypeStruct((rows, channels), narrow),
        jax.ShapeDtypeStruct((3, rows, channels), narrow),
        jax.ShapeDtypeStruct((rows, channels), full),
        jax.ShapeDtypeStruct(short_kernel.shape, full),
        jax.ShapeDtypeStruct((1, channels), full),
    )
    packed = pl.pallas_call(
        functools.partial(layer_kernel, devices),
        out_shape=packed_shapes,
        in_specs=[in_hbm] * 7,
        out_specs=(in_hbm,) * 3,
        scratch_shapes=[
            *(pltpu.VMEM(value.shape, value.dtype) for value in arguments),
            pltpu.VMEM(pair, narrow),
            pltpu.VMEM(pair, narrow),
            pltpu.VMEM(block, narrow),
            pltpu.VMEM(block, narrow),
            pltpu.VMEM(pair, narrow),
            pltpu.VMEM(block, narrow),
            pltpu.VMEM((sums_rows, LANES), full),
            pltpu.VMEM((2, extent + 2 * RIM, LANES), full),
            pltpu.VMEM((2, extent + 2 * RIM, LANES), full),
            pltpu.VMEM((extent, LANES), full),
            pltpu.VMEM((extent, LANES), full),
            pltpu.VMEM((extent, LANES), full),
            *[pltpu.VMEM((slabs // 2 + 1, rows, LANES), full)] * 3,
            pltpu.SemaphoreType.DMA((len(arguments),)),
            pltpu.SemaphoreType.DMA((3,)),
            pltpu.SemaphoreType.DMA((5, devices)),
            pltpu.SemaphoreType.DMA((5, devices)),
        ],
        compiler_params=pltpu.CompilerParams(
            collective_id=0, has_side_effects=True, vmem_limit_bytes=LIMIT
        ),
    )(*arguments)
    found = pl.pallas_call(
        unpack_kernel,
        out_shape=out_shapes,
        in_specs=[in_hbm] * 3,
        out_specs=(in_hbm,) * 5,
        scratch_shapes=[
            *(pltpu.VMEM(value.shape, value.dtype) for value in packed_shapes + out_shapes),
            pltpu.SemaphoreType.DMA((3,)),
            pltpu.SemaphoreType.DMA((5,)),
        ],
        compiler_params=pltpu.CompilerParams(vmem_limit_bytes=LIMIT),
    )(*packed)
    return (*found[:4], found[4][0])


def with_halo(block, sides, width):
    for axis, dim in sides:
        count = lax.axis_size(axis)
        forward = [(i, i + 1) for i in range(count - 1)]
        forward.append((count - 1, 0))
        backward = [(target, source) for source, target in forward]
        low = lax.ppermute(
            lax.slice_in_dim(block, block.shape[dim] - width, None, axis=dim), axis, forward
        )
        high = lax.ppermute(lax.slice_in_dim(block, 0, width, axis=dim), axis, backward)
        block = jnp.concatenate([low, block, high], axis=dim)
    return block


def dft_tables(extent):
    indices = jnp.arange(extent, dtype=jnp.int32)
    angles = (indices[:, None] * indices[None, :] % extent).astype(jnp.float32) * (
        2.0 * math.pi / extent
    )
    return (jnp.cos(angles), jnp.sin(angles))


def apply_along(matrix, signal, axis_dim):
    letters = "wxyz"
    target = letters[:axis_dim] + "k" + letters[axis_dim + 1 :]
    return jnp.einsum(
        "k" + letters[axis_dim] + "," + letters + "->" + target, matrix, signal, precision=HIGHEST
    )


def forward_section(real_part, imaginary, axis_dim):
    cosine, sine_table = dft_tables(real_part.shape[axis_dim])
    out_real = apply_along(cosine, real_part, axis_dim)
    out_imag = -apply_along(sine_table, real_part, axis_dim)
    if imaginary is not None:
        out_real = out_real + apply_along(sine_table, imaginary, axis_dim)
        out_imag = out_imag + apply_along(cosine, imaginary, axis_dim)
    return (out_real, out_imag)


def inverse_section(real_part, imaginary, axis_dim, keep_imag):
    cosine, sine_table = dft_tables(real_part.shape[axis_dim])
    out_real = apply_along(cosine, real_part, axis_dim) - apply_along(
        sine_table, imaginary, axis_dim
    )
    if keep_imag:
        return (
            out_real,
            apply_along(sine_table, real_part, axis_dim) + apply_along(cosine, imaginary, axis_dim),
        )
    return (out_real, None)


def twist(real_part, imaginary, angles, sign_factor):
    cosine = jnp.cos(angles)
    sine_table = jnp.sin(angles)
    return (
        real_part * cosine + sign_factor * imaginary * sine_table,
        imaginary * cosine - sign_factor * real_part * sine_table,
    )


def twiddle(low_index, high_index, extent):
    return (low_index * high_index % extent).astype(jnp.float32) * (2.0 * math.pi / extent)


def block_angles(devices, portion, extent):
    low_index = jnp.arange(devices, dtype=jnp.int32)[None, :, None, None]
    high_index = (lax.axis_index("seq") * portion + jnp.arange(portion, dtype=jnp.int32))[
        None, None, :, None
    ]
    return twiddle(low_index, high_index, extent)


def sequence_forward(signals, extent):
    devices = lax.axis_size("seq")
    portion = signals.shape[1] // devices
    columns = lax.all_to_all(signals[:, None], "seq", split_axis=2, concat_axis=1, tiled=True)
    real_part, imaginary = forward_section(columns, None, 1)
    real_part, imaginary = twist(real_part, imaginary, block_angles(devices, portion, extent), 1.0)
    spread = (
        lax.all_to_all(real_part, "seq", split_axis=1, concat_axis=2, tiled=True),
        lax.all_to_all(imaginary, "seq", split_axis=1, concat_axis=2, tiled=True),
    )
    return forward_section(spread[0], spread[1], 2)


def sequence_inverse(real_part, imaginary, extent):
    devices = lax.axis_size("seq")
    portion = real_part.shape[2] // devices
    real_part, imaginary = inverse_section(real_part, imaginary, 2, True)
    gathered = (
        lax.all_to_all(real_part, "seq", split_axis=2, concat_axis=1, tiled=True),
        lax.all_to_all(imaginary, "seq", split_axis=2, concat_axis=1, tiled=True),
    )
    real_part, imaginary = twist(
        gathered[0], gathered[1], block_angles(devices, portion, extent), -1.0
    )
    pieces = inverse_section(real_part, imaginary, 1, False)[0] * (1.0 / extent)
    blocks = lax.all_to_all(pieces, "seq", split_axis=1, concat_axis=2, tiled=True)
    return blocks[:, 0]


def body(projected, long_filter, short_kernel, skip_gain, cotangent):
    rows_here = projected.shape[1]
    extent = rows_here * lax.axis_size("seq")
    factor = 1.0 / math.sqrt(extent)
    kernel_span = short_kernel.shape[1]
    margin = kernel_span // 2
    padded = with_halo(projected, (("seq", 1),), margin)
    shorts = jnp.zeros(projected.shape, jnp.float32)
    for offset in range(kernel_span):
        shorts = shorts + short_kernel[:, offset][:, None, :] * padded[
            :, offset : offset + rows_here
        ].astype(jnp.float32)
    gated_signal = shorts[1] * shorts[2]
    transform, restore = (sequence_forward, sequence_inverse)
    upstream = cotangent.astype(jnp.float32)
    grad_response = upstream * shorts[0]
    spec_real, spec_imag = transform(jnp.stack([gated_signal, long_filter]), extent)
    gated_real, gated_imag = (spec_real[0], spec_imag[0])
    filter_real, filter_imag = (spec_real[1] * factor, spec_imag[1] * factor)
    product_real = filter_real * gated_real - filter_imag * gated_imag
    product_imag = filter_real * gated_imag + filter_imag * gated_real
    convolved = restore(product_real[None], product_imag[None], extent)[0]
    upstream_real, upstream_imag = transform(grad_response[None], extent)
    upstream_real, upstream_imag = (upstream_real[0], upstream_imag[0])
    back_real = jnp.stack(
        [
            filter_real * upstream_real + filter_imag * upstream_imag,
            gated_real * upstream_real + gated_imag * upstream_imag,
        ]
    )
    back_imag = jnp.stack(
        [
            filter_real * upstream_imag - filter_imag * upstream_real,
            gated_real * upstream_imag - gated_imag * upstream_real,
        ]
    )
    restored = restore(back_real, back_imag, extent)
    grad_gated = restored[0] + skip_gain * grad_response
    filter_grad = restored[1] * factor
    response = convolved + skip_gain * gated_signal
    layer_output = (response * shorts[0]).astype(jnp.bfloat16)
    grad_shorts = jnp.stack([upstream * response, grad_gated * shorts[2], grad_gated * shorts[1]])
    rimmed = with_halo(grad_shorts, (("seq", 1),), margin)
    stream_sum = jnp.zeros(grad_shorts.shape, jnp.float32)
    kernel_terms = []
    for offset in range(kernel_span):
        start_row = 2 * margin - offset
        stream_sum = (
            stream_sum
            + short_kernel[:, offset][:, None, :] * rimmed[:, start_row : start_row + rows_here]
        )
        kernel_terms.append(
            jnp.sum(
                grad_shorts * padded[:, offset : offset + rows_here].astype(jnp.float32), axis=1
            )
        )
    kernel_part = jnp.stack(kernel_terms, axis=1)
    skip_part = jnp.sum(grad_response * gated_signal, axis=0)
    kernel_total, skip_total = lax.psum((kernel_part, skip_part), "seq")
    return (
        layer_output,
        stream_sum.astype(jnp.bfloat16),
        filter_grad,
        kernel_total * factor,
        skip_total * factor,
    )


def solution(mesh):
    placed = (
        P(None, ("groups", "seq"), "chan"),
        P(("groups", "seq"), "chan"),
        P(None, None, "chan"),
        P("chan"),
        P(("groups", "seq"), "chan"),
    )
    devices = mesh.shape["seq"]

    def run(projected, *others):
        rows, channels = projected.shape[1:]
        if channels == HALF * devices and rows == LANES and devices & (devices - 1) == 0:
            return packed_body(devices, projected, *others)
        return body(projected, *others)

    return jax.shard_map(
        run,
        mesh=mesh,
        in_specs=placed,
        out_specs=(
            P(("groups", "seq"), "chan"),
            P(None, ("groups", "seq"), "chan"),
            P(("groups", "seq"), "chan"),
            P("groups", None, "chan"),
            P(("groups", "chan")),
        ),
        check_vma=False,
    )
```

```python
import functools
import math

import jax
import jax.numpy as jnp
import numpy as np
from jax import lax
from jax.experimental import pallas as pl
from jax.experimental.pallas import tpu as pltpu
from jax.sharding import PartitionSpec as P

HIGHEST = lax.Precision.HIGHEST
LANES = 128
HALF = LANES // 2
RIM = 8
LIMIT = 64 * 1024 * 1024 - 1024 * 1024


def turned(value, step, extent):
    real_part, imaginary = value
    step = step % extent
    if step == 0:
        return value
    if 2 * step == extent:
        return (-real_part, None if imaginary is None else -imaginary)
    if 4 * step == extent:
        return (None if imaginary is None else -imaginary, real_part)
    if 4 * step == 3 * extent:
        return (imaginary, -real_part)
    cosine = math.cos(2.0 * math.pi * step / extent)
    sine = math.sin(2.0 * math.pi * step / extent)
    if imaginary is None:
        return (real_part * cosine, real_part * sine)
    return (real_part * cosine - imaginary * sine, imaginary * cosine + real_part * sine)


def part_sum(left, right, sign):
    if right is None:
        return left
    if left is None:
        return right if sign > 0 else -right
    return left + right if sign > 0 else left - right


def real_spectrum(values):
    extent = len(values)
    if extent == 2:
        return [(values[0] + values[1], None), (values[0] - values[1], None)]
    even, odd = real_spectrum(values[0::2]), real_spectrum(values[1::2])
    half = extent // 2

    def entry(spectrum, index):
        index = index % half
        if 2 * index <= half:
            return spectrum[index]
        real_part, imaginary = spectrum[half - index]
        return (real_part, None if imaginary is None else -imaginary)

    found = []
    for index in range(half + 1):
        left, right = entry(even, index), turned(entry(odd, index), -index, extent)
        found.append((part_sum(left[0], right[0], 1), part_sum(left[1], right[1], 1)))
    return found


def real_values(spectrum):
    extent = 2 * (len(spectrum) - 1)
    if extent == 2:
        first, last = spectrum[0][0], spectrum[1][0]
        return [first + last, first - last]
    half = extent // 2
    even, odd = [], []
    for index in range(half // 2 + 1):
        real_part, imaginary = spectrum[index]
        if 2 * index == half:
            even.append((2.0 * real_part, None))
            odd.append((-2.0 * imaginary, None))
            continue
        other_real, other_imag = spectrum[half - index]
        even.append(
            (real_part + other_real, part_sum(imaginary, other_imag, -1))
        )
        odd.append(
            turned(
                (real_part - other_real, part_sum(imaginary, other_imag, 1)), index, extent
            )
        )
    found = [None] * extent
    found[0::2] = real_values(even)
    found[1::2] = real_values(odd)
    return found


def fine_tables(slabs, width):
    extent = slabs * width
    coarse = np.arange(slabs // 2 + 1)[:, None, None]
    fine = np.arange(width)[None, :, None]
    place = np.arange(width)[None, None, :]
    angles = ((coarse + slabs * fine) * place % extent) * (2.0 * np.pi / extent)
    cosine, sine = np.cos(angles), np.sin(angles)
    table = np.concatenate(
        [np.concatenate([cosine, sine], 2), np.concatenate([-sine, cosine], 2)], 1
    )
    inverse = np.swapaxes(table, 1, 2) / (extent * math.sqrt(extent))
    return table.astype(np.float32), inverse.astype(np.float32)


def layer_kernel(
    devices,
    projected_in,
    cotangent_in,
    filter_in,
    taps_in,
    gain_in,
    forward_in,
    inverse_in,
    recv_response,
    recv_grads,
    recv_sums,
    projected_ref,
    cotangent_ref,
    filter_ref,
    taps_ref,
    gain_ref,
    forward_ref,
    inverse_ref,
    send_pairs,
    recv_pairs,
    send_filter,
    recv_filter,
    send_grads,
    send_response,
    send_sums,
    first_rim,
    second_rim,
    first_short,
    second_short,
    signal,
    signal_spectra,
    product_spectra,
    filter_spectra,
    load_sem,
    keep_sem,
    send_sem,
    recv_sem,
):
    hops = [(devices // 2 + (-1) ** i * ((i + 1) // 2)) for i in range(devices - 1)]
    arguments = (projected_in, cotangent_in, filter_in, taps_in, gain_in, forward_in, inverse_in)
    held = (
        projected_ref,
        cotangent_ref,
        filter_ref,
        taps_ref,
        gain_ref,
        forward_ref,
        inverse_ref,
    )
    loads = [
        pltpu.make_async_copy(source, target, load_sem.at[index])
        for index, (source, target) in enumerate(zip(arguments, held))
    ]
    for load in loads:
        load.start()
    rows = projected_ref.shape[1]
    span = taps_ref.shape[1]
    margin = span // 2
    width = rows // 2
    slabs = 2 * devices
    extent = rows * devices
    factor = 1.0 / math.sqrt(extent)
    me = lax.axis_index("seq")
    odd = lax.rem(me, 2) == 1

    def low_lanes(shape):
        return lax.broadcasted_iota(jnp.int32, shape, 1) < HALF

    def swap(value):
        return pltpu.roll(value, HALF, 1)

    def join(first, second, parity):
        low = low_lanes(first.shape)
        if parity == 0:
            return jnp.where(low, first, swap(second))
        return jnp.where(low, swap(first), second)

    def wide(value):
        return value.astype(jnp.float32)

    def copy_to(kind, hop, source, target, slot, peer):
        return pltpu.make_async_remote_copy(
            src_ref=source,
            dst_ref=target.at[slot],
            send_sem=send_sem.at[kind, hop],
            recv_sem=recv_sem.at[kind, hop],
            device_id={"seq": peer},
            device_id_type=pl.DeviceIdType.MESH,
        )

    def peer_at(hop):
        return lax.rem(me + hop, devices)

    def source_at(hop):
        return lax.rem(me + devices - hop, devices)

    barrier = pltpu.get_barrier_semaphore()
    for hop in hops:
        pl.semaphore_signal(
            barrier, inc=1, device_id={"seq": peer_at(hop)}, device_id_type=pl.DeviceIdType.MESH
        )

    loads[0].wait()
    loads[1].wait()
    def lanes_of(peer):
        return pl.ds(pl.multiple_of((peer // 2) * LANES, LANES), LANES)

    def join_for(peer, first, second):
        flip = lax.rem(peer, 2) == 1
        return jnp.where(
            low_lanes(first.shape),
            jnp.where(flip, swap(first), first),
            jnp.where(flip, second, swap(second)),
        ).astype(jnp.bfloat16)

    def pack_pairs(peer, target):
        lanes = lanes_of(peer)
        gate, left, right = [wide(projected_ref[s, :, lanes]) for s in range(3)]
        target[0] = join_for(peer, left, gate)
        target[1] = join_for(peer, right, wide(cotangent_ref[:, lanes]))

    def pack_filter(peer, target):
        whole = filter_ref[:, lanes_of(peer)]
        coarse = wide(whole.astype(jnp.bfloat16))
        target[...] = join_for(peer, coarse, whole - coarse)

    for place, hop in enumerate(hops):
        peer = peer_at(hop)
        pack_pairs(peer, send_pairs.at[peer])
        if place == 0:
            pl.semaphore_wait(barrier, devices - 1)
        copy_to(0, hop, send_pairs.at[peer], recv_pairs, me, peer).start()
    loads[2].wait()
    for hop in hops:
        peer = peer_at(hop)
        pack_filter(peer, send_filter.at[peer])
        copy_to(1, hop, send_filter.at[peer], recv_filter, me, peer).start()
    pack_pairs(me, recv_pairs.at[me])
    pack_filter(me, recv_filter.at[me])

    for load in loads[3:5]:
        load.wait()
    own = pl.ds(pl.multiple_of((me // 2) * LANES, LANES), LANES)

    def own_pair(first, second):
        return jnp.where(odd, join(first, second, 1), join(first, second, 0))

    gate_taps, left_taps, right_taps = [taps_ref[s, :, own] for s in range(3)]
    first_taps = own_pair(left_taps, gate_taps)
    centre = wide(lax.broadcasted_iota(jnp.int32, (span, LANES), 0) == margin)
    second_taps = jnp.where(
        low_lanes((span, LANES)), own_pair(right_taps, right_taps), centre
    )
    own_gain = gain_ref[:, own]
    gain = own_pair(own_gain, own_gain)

    def wait_from(kind, source, target):
        for hop in hops:
            copy_to(kind, hop, source.at[peer_at(hop)], target, source_at(hop), peer_at(hop)).wait()

    def close_rim(rim):
        rim[0:RIM] = rim[extent : extent + RIM]
        rim[extent + RIM : extent + 2 * RIM] = rim[RIM : 2 * RIM]

    wait_from(0, send_pairs, recv_pairs)
    for block in range(devices):
        here = slice(RIM + block * rows, RIM + (block + 1) * rows)
        first_rim[0, here] = wide(recv_pairs[block, 0])
        second_rim[0, here] = wide(recv_pairs[block, 1])
    close_rim(first_rim.at[0])
    close_rim(second_rim.at[0])

    def shorten(slab, total):
        start = pl.multiple_of(slab * width, width)
        around_first = first_rim[0, pl.ds(start, width + 2 * RIM)]
        around_second = second_rim[0, pl.ds(start, width + 2 * RIM)]
        first = jnp.zeros((width, LANES), jnp.float32)
        second = jnp.zeros((width, LANES), jnp.float32)
        for tap in range(span):
            low = RIM + tap - margin
            first = first + first_taps[tap : tap + 1] * around_first[low : low + width]
            second = second + second_taps[tap : tap + 1] * around_second[low : low + width]
        product = first * second
        first_short[pl.ds(start, width)] = first
        second_short[pl.ds(start, width)] = second
        signal[pl.ds(start, width)] = product
        return total + jnp.sum((product * swap(product)).reshape(-1, 8, LANES), axis=0)

    gain_sum = lax.fori_loop(0, slabs, shorten, jnp.zeros((8, LANES), jnp.float32))

    def put_spectrum(spectra, found, start, count):
        for index, (real_part, imaginary) in enumerate(found):
            if imaginary is None:
                imaginary = jnp.zeros_like(real_part)
            spectra[index, pl.ds(start, count)] = real_part
            spectra[index, pl.ds(width + start, count)] = imaginary

    def signal_spectrum(step, carry):
        start = pl.multiple_of(step * 8, 8)
        values = [signal[pl.ds(slab * width + start, 8)] for slab in range(slabs)]
        put_spectrum(signal_spectra, real_spectrum(values), start, 8)
        return carry

    lax.fori_loop(0, width // 8, signal_spectrum, 0)

    for load in loads[5:]:
        load.wait()
    sign = jnp.where(low_lanes((width, LANES)), 1.0, -1.0).astype(jnp.float32)
    for index in range(slabs // 2 + 1):
        found = jnp.dot(forward_ref[index], signal_spectra[index], precision=HIGHEST)
        signal_spectra[index] = found
        real_part, imaginary = found[:width], found[width:]
        other_real, other_imag = swap(real_part), swap(imaginary)
        product = jnp.concatenate(
            [
                real_part * other_real + imaginary * other_imag,
                sign * (real_part * other_imag - imaginary * other_real),
            ],
            axis=0,
        )
        product_spectra[index] = jnp.dot(inverse_ref[index], product, precision=HIGHEST)

    def get_spectrum(spectra, start, count):
        found = []
        for index in range(slabs // 2 + 1):
            imaginary = None
            if 0 < index < slabs // 2:
                imaginary = spectra[index, pl.ds(width + start, count)]
            found.append((spectra[index, pl.ds(start, count)], imaginary))
        return found

    def filter_back(step, carry):
        start = pl.multiple_of(step * 16, 16)
        values = real_values(get_spectrum(product_spectra, start, 16))
        low = low_lanes((16, LANES))
        for slab, value in enumerate(values):
            coarse = wide(value.astype(jnp.bfloat16))
            send_response[slab // 2, pl.ds((slab % 2) * width + start, 16)] = jnp.where(
                low, coarse, value - coarse
            ).astype(jnp.bfloat16)
        return carry

    lax.fori_loop(0, width // 16, filter_back, 0)
    for hop in hops:
        peer = peer_at(hop)
        copy_to(2, hop, send_response.at[peer], recv_response, me, peer).start()
    kept = [
        pltpu.make_async_copy(source, target.at[me], keep_sem.at[index])
        for index, (source, target) in enumerate(
            (
                (send_response.at[me], recv_response),
                (send_grads.at[me], recv_grads),
                (send_sums, recv_sums),
            )
        )
    ]
    kept[0].start()

    wait_from(1, send_filter, recv_filter)

    def filter_spectrum(step, carry):
        start = pl.multiple_of(step * 16, 16)
        values = []
        for slab in range(slabs):
            packed = wide(recv_filter[slab // 2, pl.ds((slab % 2) * width + start, 16)])
            values.append(packed + swap(packed))
        put_spectrum(filter_spectra, real_spectrum(values), start, 16)
        return carry

    lax.fori_loop(0, width // 16, filter_spectrum, 0)

    for index in range(slabs // 2 + 1):
        found = jnp.dot(forward_ref[index], filter_spectra[index], precision=HIGHEST)
        filter_real, filter_imag = found[:width], sign * found[width:]
        real_part, imaginary = signal_spectra[index, :width], signal_spectra[index, width:]
        product = jnp.concatenate(
            [
                filter_real * real_part - filter_imag * imaginary,
                filter_real * imaginary + filter_imag * real_part,
            ],
            axis=0,
        )
        filter_spectra[index] = jnp.dot(inverse_ref[index], product, precision=HIGHEST)

    def signal_back(step, carry):
        start = pl.multiple_of(step * 8, 8)
        values = real_values(get_spectrum(filter_spectra, start, 8))
        for slab, value in enumerate(values):
            place = pl.ds(slab * width + start, 8)
            back = swap(value + gain * signal[place])
            inner = pl.ds(RIM + slab * width + start, 8)
            first_rim[1, inner] = back * second_short[place]
            second_rim[1, inner] = back * first_short[place]
        return carry

    lax.fori_loop(0, width // 8, signal_back, 0)
    close_rim(first_rim.at[1])
    close_rim(second_rim.at[1])

    def grads(block, sums):
        sums = list(sums)
        for part in range(2):
            start = pl.multiple_of(block * rows + part * width, width)
            inner = pl.ds(start, width + 2 * RIM)
            for which, (rim, taps) in enumerate(((first_rim, first_taps), (second_rim, second_taps))):
                around = rim[1, inner]
                streams = rim[0, inner]
                here = around[RIM : RIM + width]
                total = jnp.zeros((width, LANES), jnp.float32)
                for tap in range(span):
                    low = RIM + margin - tap
                    total = total + taps[tap : tap + 1] * around[low : low + width]
                    low = RIM + tap - margin
                    sums[which * span + tap] = sums[which * span + tap] + jnp.sum(
                        (here * streams[low : low + width]).reshape(-1, 8, LANES), axis=0
                    )
                send_grads[block, which, part * width : (part + 1) * width] = total.astype(
                    jnp.bfloat16
                )
        return tuple(sums)

    def step_grads(step, sums):
        hop = devices // 2 + (step + 1) // 2 * (1 - 2 * lax.rem(step, 2))
        peer = peer_at(hop)
        sums = grads(peer, sums)
        copy_to(3, hop, send_grads.at[peer], recv_grads, me, peer).start()
        return sums

    sums = tuple(jnp.zeros((8, LANES), jnp.float32) for _ in range(2 * span))
    sums = lax.fori_loop(0, devices - 1, step_grads, sums)
    sums = grads(me, sums)
    sums = [factor * jnp.sum(value, axis=0, keepdims=True) for value in sums + (gain_sum,)]
    middle = (span + 1) // 2
    for index in range(span):
        send_sums[index : index + 1] = sums[index]
    for index in range(span, span + middle):
        send_sums[index : index + 1] = join(sums[index], sums[index + middle], 0)
    for hop in hops:
        copy_to(4, hop, send_sums, recv_sums, me, peer_at(hop)).start()
    kept[1].start()
    kept[2].start()
    for keep in kept:
        keep.wait()
    wait_from(2, send_response, recv_response)
    wait_from(3, send_grads, recv_grads)
    for hop in hops:
        copy_to(4, hop, send_sums, recv_sums, source_at(hop), peer_at(hop)).wait()


def unpack_kernel(*refs):
    packed, results, held, refs = refs[:3], refs[3:8], refs[8:11], refs[11:]
    output_ref, streams_ref, filter_grad_ref, taps_grad_ref, gain_grad_ref = refs[:5]
    recv_response, recv_grads, recv_sums = held
    load_sem, store_sem = refs[5:]
    loads = [pltpu.make_async_copy(packed[i], held[i], load_sem.at[i]) for i in range(3)]
    stores = [pltpu.make_async_copy(refs[i], results[i], store_sem.at[i]) for i in range(5)]
    for load in loads:
        load.start()
    tiles = recv_response.shape[0] // 2
    span = taps_grad_ref.shape[1]
    middle = (span + 1) // 2

    def low_lanes(shape):
        return lax.broadcasted_iota(jnp.int32, shape, 1) < HALF

    def swap(value):
        return pltpu.roll(value, HALF, 1)

    def wide(value):
        return value.astype(jnp.float32)

    def split(first, second):
        low = low_lanes(first.shape)
        return jnp.where(low, first, swap(second)), jnp.where(low, swap(first), second)

    loads[0].wait()
    for tile in range(tiles):
        lanes = slice(tile * LANES, (tile + 1) * LANES)
        first, second = wide(recv_response[2 * tile]), wide(recv_response[2 * tile + 1])
        filter_grad_ref[:, lanes] = jnp.where(
            low_lanes(first.shape), first + swap(first), second + swap(second)
        )
    stores[2].start()
    loads[1].wait()
    for tile in range(tiles):
        lanes = slice(tile * LANES, (tile + 1) * LANES)
        for which, targets in enumerate(
            ((streams_ref.at[1], streams_ref.at[0]), (streams_ref.at[2], output_ref))
        ):
            pieces = split(wide(recv_grads[2 * tile, which]), wide(recv_grads[2 * tile + 1, which]))
            for target, piece in zip(targets, pieces):
                target[:, lanes] = piece.astype(jnp.bfloat16)
    stores[0].start()
    stores[1].start()
    loads[2].wait()
    for tile in range(tiles):
        lanes = slice(tile * LANES, (tile + 1) * LANES)
        low_part, high_part = split(recv_sums[2 * tile], recv_sums[2 * tile + 1])
        taps_grad_ref[1, :, lanes] = low_part[0:span]
        taps_grad_ref[0, :, lanes] = high_part[0:span]
        taps_grad_ref[2, :middle, lanes] = low_part[span:]
        taps_grad_ref[2, middle:, lanes] = high_part[span : 2 * span - middle]
        gain_grad_ref[:, lanes] = high_part[2 * span - middle : 2 * span - middle + 1]
    stores[3].start()
    stores[4].start()
    for store in stores:
        store.wait()


def packed_body(devices, projected, long_filter, short_kernel, skip_gain, cotangent):
    rows, channels = long_filter.shape
    span = short_kernel.shape[1]
    extent = rows * devices
    slabs = 2 * devices
    tables = fine_tables(slabs, rows // 2)
    sums_rows = span + (span + 1) // 2
    block = (devices, rows, LANES)
    pair = (devices, 2, rows, LANES)
    narrow, full = jnp.bfloat16, jnp.float32
    arguments = (projected, cotangent, long_filter, short_kernel, skip_gain[None], *tables)
    in_hbm = pl.BlockSpec(memory_space=pltpu.HBM)
    packed_shapes = (
        jax.ShapeDtypeStruct(block, narrow),
        jax.ShapeDtypeStruct(pair, narrow),
        jax.ShapeDtypeStruct((devices, sums_rows, LANES), full),
    )
    out_shapes = (
        jax.ShapeDtypeStruct((rows, channels), narrow),
        jax.ShapeDtypeStruct((3, rows, channels), narrow),
        jax.ShapeDtypeStruct((rows, channels), full),
        jax.ShapeDtypeStruct(short_kernel.shape, full),
        jax.ShapeDtypeStruct((1, channels), full),
    )
    packed = pl.pallas_call(
        functools.partial(layer_kernel, devices),
        out_shape=packed_shapes,
        in_specs=[in_hbm] * 7,
        out_specs=(in_hbm,) * 3,
        scratch_shapes=[
            *(pltpu.VMEM(value.shape, value.dtype) for value in arguments),
            pltpu.VMEM(pair, narrow),
            pltpu.VMEM(pair, narrow),
            pltpu.VMEM(block, narrow),
            pltpu.VMEM(block, narrow),
            pltpu.VMEM(pair, narrow),
            pltpu.VMEM(block, narrow),
            pltpu.VMEM((sums_rows, LANES), full),
            pltpu.VMEM((2, extent + 2 * RIM, LANES), full),
            pltpu.VMEM((2, extent + 2 * RIM, LANES), full),
            pltpu.VMEM((extent, LANES), full),
            pltpu.VMEM((extent, LANES), full),
            pltpu.VMEM((extent, LANES), full),
            *[pltpu.VMEM((slabs // 2 + 1, rows, LANES), full)] * 3,
            pltpu.SemaphoreType.DMA((len(arguments),)),
            pltpu.SemaphoreType.DMA((3,)),
            pltpu.SemaphoreType.DMA((5, devices)),
            pltpu.SemaphoreType.DMA((5, devices)),
        ],
        compiler_params=pltpu.CompilerParams(
            collective_id=0, has_side_effects=True, vmem_limit_bytes=LIMIT
        ),
    )(*arguments)
    found = pl.pallas_call(
        unpack_kernel,
        out_shape=out_shapes,
        in_specs=[in_hbm] * 3,
        out_specs=(in_hbm,) * 5,
        scratch_shapes=[
            *(pltpu.VMEM(value.shape, value.dtype) for value in packed_shapes + out_shapes),
            pltpu.SemaphoreType.DMA((3,)),
            pltpu.SemaphoreType.DMA((5,)),
        ],
        compiler_params=pltpu.CompilerParams(vmem_limit_bytes=LIMIT),
    )(*packed)
    return (*found[:4], found[4][0])


def with_halo(block, sides, width):
    for axis, dim in sides:
        count = lax.axis_size(axis)
        forward = [(i, i + 1) for i in range(count - 1)]
        forward.append((count - 1, 0))
        backward = [(target, source) for source, target in forward]
        low = lax.ppermute(
            lax.slice_in_dim(block, block.shape[dim] - width, None, axis=dim), axis, forward
        )
        high = lax.ppermute(lax.slice_in_dim(block, 0, width, axis=dim), axis, backward)
        block = jnp.concatenate([low, block, high], axis=dim)
    return block


def dft_tables(extent):
    indices = jnp.arange(extent, dtype=jnp.int32)
    angles = (indices[:, None] * indices[None, :] % extent).astype(jnp.float32) * (
        2.0 * math.pi / extent
    )
    return (jnp.cos(angles), jnp.sin(angles))


def apply_along(matrix, signal, axis_dim):
    letters = "wxyz"
    target = letters[:axis_dim] + "k" + letters[axis_dim + 1 :]
    return jnp.einsum(
        "k" + letters[axis_dim] + "," + letters + "->" + target, matrix, signal, precision=HIGHEST
    )


def forward_section(real_part, imaginary, axis_dim):
    cosine, sine_table = dft_tables(real_part.shape[axis_dim])
    out_real = apply_along(cosine, real_part, axis_dim)
    out_imag = -apply_along(sine_table, real_part, axis_dim)
    if imaginary is not None:
        out_real = out_real + apply_along(sine_table, imaginary, axis_dim)
        out_imag = out_imag + apply_along(cosine, imaginary, axis_dim)
    return (out_real, out_imag)


def inverse_section(real_part, imaginary, axis_dim, keep_imag):
    cosine, sine_table = dft_tables(real_part.shape[axis_dim])
    out_real = apply_along(cosine, real_part, axis_dim) - apply_along(
        sine_table, imaginary, axis_dim
    )
    if keep_imag:
        return (
            out_real,
            apply_along(sine_table, real_part, axis_dim) + apply_along(cosine, imaginary, axis_dim),
        )
    return (out_real, None)


def twist(real_part, imaginary, angles, sign_factor):
    cosine = jnp.cos(angles)
    sine_table = jnp.sin(angles)
    return (
        real_part * cosine + sign_factor * imaginary * sine_table,
        imaginary * cosine - sign_factor * real_part * sine_table,
    )


def twiddle(low_index, high_index, extent):
    return (low_index * high_index % extent).astype(jnp.float32) * (2.0 * math.pi / extent)


def block_angles(devices, portion, extent):
    low_index = jnp.arange(devices, dtype=jnp.int32)[None, :, None, None]
    high_index = (lax.axis_index("seq") * portion + jnp.arange(portion, dtype=jnp.int32))[
        None, None, :, None
    ]
    return twiddle(low_index, high_index, extent)


def sequence_forward(signals, extent):
    devices = lax.axis_size("seq")
    portion = signals.shape[1] // devices
    columns = lax.all_to_all(signals[:, None], "seq", split_axis=2, concat_axis=1, tiled=True)
    real_part, imaginary = forward_section(columns, None, 1)
    real_part, imaginary = twist(real_part, imaginary, block_angles(devices, portion, extent), 1.0)
    spread = (
        lax.all_to_all(real_part, "seq", split_axis=1, concat_axis=2, tiled=True),
        lax.all_to_all(imaginary, "seq", split_axis=1, concat_axis=2, tiled=True),
    )
    return forward_section(spread[0], spread[1], 2)


def sequence_inverse(real_part, imaginary, extent):
    devices = lax.axis_size("seq")
    portion = real_part.shape[2] // devices
    real_part, imaginary = inverse_section(real_part, imaginary, 2, True)
    gathered = (
        lax.all_to_all(real_part, "seq", split_axis=2, concat_axis=1, tiled=True),
        lax.all_to_all(imaginary, "seq", split_axis=2, concat_axis=1, tiled=True),
    )
    real_part, imaginary = twist(
        gathered[0], gathered[1], block_angles(devices, portion, extent), -1.0
    )
    pieces = inverse_section(real_part, imaginary, 1, False)[0] * (1.0 / extent)
    blocks = lax.all_to_all(pieces, "seq", split_axis=1, concat_axis=2, tiled=True)
    return blocks[:, 0]


def body(projected, long_filter, short_kernel, skip_gain, cotangent):
    rows_here = projected.shape[1]
    extent = rows_here * lax.axis_size("seq")
    factor = 1.0 / math.sqrt(extent)
    kernel_span = short_kernel.shape[1]
    margin = kernel_span // 2
    padded = with_halo(projected, (("seq", 1),), margin)
    shorts = jnp.zeros(projected.shape, jnp.float32)
    for offset in range(kernel_span):
        shorts = shorts + short_kernel[:, offset][:, None, :] * padded[
            :, offset : offset + rows_here
        ].astype(jnp.float32)
    gated_signal = shorts[1] * shorts[2]
    transform, restore = (sequence_forward, sequence_inverse)
    upstream = cotangent.astype(jnp.float32)
    grad_response = upstream * shorts[0]
    spec_real, spec_imag = transform(jnp.stack([gated_signal, long_filter]), extent)
    gated_real, gated_imag = (spec_real[0], spec_imag[0])
    filter_real, filter_imag = (spec_real[1] * factor, spec_imag[1] * factor)
    product_real = filter_real * gated_real - filter_imag * gated_imag
    product_imag = filter_real * gated_imag + filter_imag * gated_real
    convolved = restore(product_real[None], product_imag[None], extent)[0]
    upstream_real, upstream_imag = transform(grad_response[None], extent)
    upstream_real, upstream_imag = (upstream_real[0], upstream_imag[0])
    back_real = jnp.stack(
        [
            filter_real * upstream_real + filter_imag * upstream_imag,
            gated_real * upstream_real + gated_imag * upstream_imag,
        ]
    )
    back_imag = jnp.stack(
        [
            filter_real * upstream_imag - filter_imag * upstream_real,
            gated_real * upstream_imag - gated_imag * upstream_real,
        ]
    )
    restored = restore(back_real, back_imag, extent)
    grad_gated = restored[0] + skip_gain * grad_response
    filter_grad = restored[1] * factor
    response = convolved + skip_gain * gated_signal
    layer_output = (response * shorts[0]).astype(jnp.bfloat16)
    grad_shorts = jnp.stack([upstream * response, grad_gated * shorts[2], grad_gated * shorts[1]])
    rimmed = with_halo(grad_shorts, (("seq", 1),), margin)
    stream_sum = jnp.zeros(grad_shorts.shape, jnp.float32)
    kernel_terms = []
    for offset in range(kernel_span):
        start_row = 2 * margin - offset
        stream_sum = (
            stream_sum
            + short_kernel[:, offset][:, None, :] * rimmed[:, start_row : start_row + rows_here]
        )
        kernel_terms.append(
            jnp.sum(
                grad_shorts * padded[:, offset : offset + rows_here].astype(jnp.float32), axis=1
            )
        )
    kernel_part = jnp.stack(kernel_terms, axis=1)
    skip_part = jnp.sum(grad_response * gated_signal, axis=0)
    kernel_total, skip_total = lax.psum((kernel_part, skip_part), "seq")
    return (
        layer_output,
        stream_sum.astype(jnp.bfloat16),
        filter_grad,
        kernel_total * factor,
        skip_total * factor,
    )


def solution(mesh):
    placed = (
        P(None, ("groups", "seq"), "chan"),
        P(("groups", "seq"), "chan"),
        P(None, None, "chan"),
        P("chan"),
        P(("groups", "seq"), "chan"),
    )
    devices = mesh.shape["seq"]

    def run(projected, *others):
        rows, channels = projected.shape[1:]
        if channels == HALF * devices and rows == LANES and devices & (devices - 1) == 0:
            return packed_body(devices, projected, *others)
        return body(projected, *others)

    return jax.shard_map(
        run,
        mesh=mesh,
        in_specs=placed,
        out_specs=(
            P(("groups", "seq"), "chan"),
            P(None, ("groups", "seq"), "chan"),
            P(("groups", "seq"), "chan"),
            P("groups", None, "chan"),
            P(("groups", "chan")),
        ),
        check_vma=False,
    )
```
